128 devices in a mesh: dp: 16 (over y_hi, x, core), hid: 8 (over y_lo, z).
Axes of the slice: x: 4, y: 4 (y_hi: 2, y_lo: 2; y = y_hi * 2 + y_lo), z: 4, core: 2. Of those that a mesh axis runs over, the one named last changes fastest.
Arguments:
- train_x: bfloat16 [4096, 4096], P('dp', 'hid'), may hold values from -6 to 6
- gate_pre: bfloat16 [4096, 14336], P('dp', 'hid'), may hold values from -6 to 6
- up_pre: bfloat16 [4096, 14336], P('dp', 'hid'), may hold values from -6 to 6
- train_dy: bfloat16 [4096, 4096], P('dp'), may hold values from -6 to 6
- val_x: bfloat16 [512, 4096], P('dp', 'hid'), may hold values from -6 to 6
- val_gate: bfloat16 [512, 14336], P('dp', 'hid'), may hold values from -6 to 6
- val_up: bfloat16 [512, 14336], P('dp', 'hid'), may hold values from -6 to 6
- val_dy: bfloat16 [512, 4096], P('dp'), may hold values from -6 to 6
- down_weight: bfloat16 [14336, 4096], P('hid', 'dp'), may hold values from -0.046875 to 0.046875
Outputs:
- gate_grad: bfloat16 [4096, 14336], P('dp', 'hid')
- up_grad: bfloat16 [4096, 14336], P('dp', 'hid')
- scores: float32 [16, 2], P('dp')
The draws below stay inside these ranges and needn't reach their ends.
All inputs are finite; a program needn't handle non-finite values.
Results may differ from the reference program's by a relative error of at most 0.0059.
Values may be sent and summed in bfloat16 or wider, within the bound.
A program may use at most 128 MiB of HBM per device.

```python
import jax
import jax.numpy as jnp
from jax import lax

D = 4096
FF = 14336
LEN = 256
NTRAIN = 16
TOKENS = 4096
VTOK = 512
NVAL = 2


def level_of(rng, shape, cuts, low, high):
    level = 1.0
    for dim, blocks in cuts:
        steps = jax.random.uniform(jax.random.fold_in(jax.random.fold_in(rng, 6), dim), (blocks,), jnp.float32, low / len(cuts), high / len(cuts))
        level = level * jnp.repeat(jnp.exp(steps), shape[dim] // blocks).reshape((-1,) + (1,) * (len(shape) - 1 - dim))
    return level


def scatter_about(stream_key, shape, deviation, most, shards=(), kind=jnp.bfloat16):
    values = deviation * jax.random.normal(stream_key, shape, jnp.float32)
    if shards:
        values = values * level_of(stream_key, shape, shards, -0.22, 0.18)
    return jnp.clip(values, -most, most).astype(kind)


def setup_inputs(seed: int = 0) -> dict:
    key_list = jax.random.split(jax.random.key(seed), 10)
    return {
        "train_x": scatter_about(key_list[0], (TOKENS, D), 1.0, 6.0, ((0, 16), (1, 8))),
        "gate_pre": scatter_about(key_list[1], (TOKENS, FF), 1.0, 6.0, ((0, 16), (1, 8))),
        "up_pre": scatter_about(key_list[2], (TOKENS, FF), 1.0, 6.0, ((0, 16), (1, 8))),
        "train_dy": scatter_about(key_list[3], (TOKENS, D), 1.0, 6.0, ((0, 16),)),
        "val_x": scatter_about(key_list[4], (VTOK, D), 1.0, 6.0, ((0, 16), (1, 8))),
        "val_gate": scatter_about(key_list[5], (VTOK, FF), 1.0, 6.0, ((0, 16), (1, 8))),
        "val_up": scatter_about(key_list[6], (VTOK, FF), 1.0, 6.0, ((0, 16), (1, 8))),
        "val_dy": scatter_about(key_list[7], (VTOK, D), 1.0, 6.0, ((0, 16),)),
        "down_weight": scatter_about(key_list[8], (FF, D), FF ** -0.5, 0.046875, ((0, 8), (1, 16))),
    }


step_rate = 0.1


def backward_parts(hidden_cot, gate, up):
    a = gate.astype(jnp.float32)
    b = up.astype(jnp.float32)
    s = jax.nn.sigmoid(a)
    silu = a * s
    hidden = (silu * b).astype(jnp.bfloat16)
    gate_grad = (hidden_cot * b * s * (1.0 + a * (1.0 - s))).astype(jnp.bfloat16)
    up_grad = (hidden_cot * silu).astype(jnp.bfloat16)
    return hidden, gate_grad, up_grad


def pair_dot(left, right):
    return lax.dot_general(left, right, (((1,), (1,)), ((), ())), preferred_element_type=jnp.float32)


def reference(train_x, gate_pre, up_pre, train_dy, val_x, val_gate, val_up, val_dy, down_weight):
    cot_train = pair_dot(train_dy, down_weight)
    cot_val = pair_dot(val_dy, down_weight)
    hidden, gate_grad, up_grad = backward_parts(cot_train, gate_pre, up_pre)
    val_hidden, val_gate_grad, val_up_grad = backward_parts(cot_val, val_gate, val_up)
    train_g = jnp.concatenate([gate_grad, up_grad], axis=1)
    val_g = jnp.concatenate([val_gate_grad, val_up_grad], axis=1)

    def one_val(index):
        begin = (index * LEN).astype(jnp.int32)
        vx = lax.dynamic_slice_in_dim(val_x, begin, LEN, 0)
        vg = lax.dynamic_slice_in_dim(val_g, begin, LEN, 0)
        vh = lax.dynamic_slice_in_dim(val_hidden, begin, LEN, 0)
        vy = lax.dynamic_slice_in_dim(val_dy, begin, LEN, 0)
        pair = pair_dot(train_x, vx) * pair_dot(train_g, vg) + pair_dot(hidden, vh) * pair_dot(train_dy, vy)
        per_token = jnp.sum(pair, axis=1)
        return jnp.sum(per_token.reshape(NTRAIN, LEN), axis=1)

    columns = lax.map(one_val, jnp.arange(NVAL, dtype=jnp.int32))
    scores = columns.T * (-step_rate / (LEN * LEN))
    return gate_grad, up_grad, scores
```

```python
import functools

import jax
import jax.numpy as jnp
from jax import lax
from jax.experimental import pallas as pl
from jax.experimental.pallas import tpu as pltpu
from jax.sharding import PartitionSpec as P

LEN = 256
step_rate = 0.1
MESH = pl.DeviceIdType.MESH
BF = jnp.bfloat16
F32 = jnp.float32

TOK = 256
VAL = 32
FFL = 1792
FC = 256
NC = FFL // FC
KH = 2048
BW = 64


def dot_t(a, b):
    return lax.dot_general(a, b, (((1,), (1,)), ((), ())), preferred_element_type=F32)


def parts(cot, gate, up):
    a = gate.astype(F32)
    b = up.astype(F32)
    s = jax.nn.sigmoid(a)
    silu = a * s
    hidden = (silu * b).astype(BF)
    gate_grad = (cot * b * s * (1.0 + a * (1.0 - s))).astype(BF)
    up_grad = (cot * silu).astype(BF)
    return hidden, gate_grad, up_grad


def kernel(
    tx_h, gate_h, up_h, dy_h, vx_h, vg_h, vu_h, vdy_h, w_h,
    gg_o, ug_o, sc_o,
    wbuf, lhs, tx, tdy, gate, up, e1, vg, vu, vc, ownp, psend, precv, gg, ug, hd,
    iop, ior, ios, ioy, iof, cacc, hacc, fin_s, fin_r,
    lsem, osem, ring_s, ring_r, y_s, y_r, p_s, p_r, z_s, z_r, f_s, f_r,
):
    i_dp = lax.axis_index("dp")
    i_hid = lax.axis_index("hid")
    yh, x, k = i_dp // 8, (i_dp // 2) % 4, i_dp % 2
    yl, z = i_hid // 4, i_hid % 4
    xm, xp, x2 = (x + 3) % 4, (x + 1) % 4, (x + 2) % 4

    def dev(yh_=yh, x_=x, k_=k, yl_=yl, z_=z):
        return ((yh_ * 4 + x_) * 2 + k_, yl_ * 4 + z_)

    right, left, sib = dev(x_=xp), dev(x_=xm), dev(k_=1 - k)
    ypart, cross, ylp = dev(yh_=1 - yh), dev(yh_=1 - yh, yl_=1 - yl), dev(yl_=1 - yl)
    zdev = [dev(z_=(z + d) % 4) for d in (1, 2, 3)]
    hids = zdev + [dev(yl_=1 - yl, z_=(z + d) % 4) for d in range(4)]

    def remote(src, dst, ss, rs, to):
        return pltpu.make_async_remote_copy(
            src_ref=src, dst_ref=dst, send_sem=ss, recv_sem=rs, device_id=to, device_id_type=MESH
        )

    me_blk = x * 2 + k
    own_rows = pl.ds(pl.multiple_of(me_blk * BW + yh * VAL, VAL), VAL)
    half_cols = pl.ds(pl.multiple_of(yh * KH, KH), KH)
    hid_cols = pl.ds(pl.multiple_of(i_hid * 512, 512), 512)
    wcol = pl.ds(pl.multiple_of(me_blk * 256, 256), 256)
    local = [
        (w_h, wbuf.at[:, wcol]),
        (vx_h, e1.at[own_rows, pl.ds(0, 512)]),
        (vdy_h.at[:, hid_cols], e1.at[own_rows, pl.ds(512, 512)]),
        (vg_h, vg.at[own_rows, :]),
        (vu_h, vu.at[own_rows, :]),
        (dy_h.at[:, half_cols], lhs.at[pl.ds(0, TOK), :]),
        (vdy_h.at[:, half_cols], lhs.at[pl.ds(TOK, VAL), :]),
        (tx_h, tx),
        (dy_h.at[:, hid_cols], tdy),
        (gate_h, gate),
        (up_h, up),
    ]
    local = [pltpu.make_async_copy(a, b, lsem.at[n]) for n, (a, b) in enumerate(local)]
    for cp in local:
        cp.start()

    barrier = pltpu.get_barrier_semaphore()
    greet = [right, left, sib, ypart, cross] + hids
    for to in greet:
        pl.semaphore_signal(barrier, inc=1, device_id=to, device_id_type=MESH)
    pl.semaphore_wait(barrier, len(greet))

    class Ring:
        def __init__(self, slot, view, half):
            self.slot, self.view, self.half = slot, view, half

        def cp(self, n, ref, to):
            return remote(ref, ref, ring_s.at[self.slot, n], ring_r.at[self.slot, n], to)

        def own(self, src=None):
            for n, to in ((0, right), (1, left), (4, sib)):
                ref = self.view(x, k)
                remote(
                    ref if src is None else src, ref,
                    ring_s.at[self.slot, n], ring_r.at[self.slot, n], to,
                ).start()

        def forward(self):
            self.cp(0, self.view(xm, k), right).wait_recv()
            self.cp(2, self.half(xm, k, 0), right).start()
            self.cp(5, self.view(xm, k), sib).start()
            self.cp(1, self.view(xp, k), left).wait_recv()
            self.cp(3, self.half(xp, k, 1), left).start()
            self.cp(6, self.view(xp, k), sib).start()

        def last(self):
            self.cp(2, self.half(x2, k, 0), right).wait_recv()
            self.cp(3, self.half(x2, k, 1), left).wait_recv()
            self.cp(7, self.view(x2, k), sib).start()

        def full(self):
            for n, xx in ((4, x), (5, xm), (6, xp), (7, x2)):
                self.cp(n, self.view(xx, 1 - k), sib).wait_recv()

        def drain(self):
            for n in (0, 1, 4, 5, 6, 7):
                self.cp(n, self.view(x, k), sib).wait_send()
            for n in (2, 3):
                self.cp(n, self.half(x, k, 0), sib).wait_send()

    def wring(s):
        def view(xx, kk):
            return wbuf.at[
                pl.ds(pl.multiple_of(s * FC, FC), FC),
                pl.ds(pl.multiple_of((xx * 2 + kk) * 256, 256), 256),
            ]

        def half(xx, kk, n):
            return wbuf.at[
                pl.ds(pl.multiple_of(s * FC + n * (FC // 2), FC // 2), FC // 2),
                pl.ds(pl.multiple_of((xx * 2 + kk) * 256, 256), 256),
            ]

        return Ring(s, view, half)

    def vring(slot, buf, first, width):
        def rows(xx, kk):
            return pl.ds(pl.multiple_of((xx * 2 + kk) * BW, BW), BW)

        def view(xx, kk):
            return buf.at[rows(xx, kk), pl.ds(first, width)]

        def half(xx, kk, n):
            return buf.at[rows(xx, kk), pl.ds(first + n * (width // 2), width // 2)]

        return Ring(slot, view, half)

    def vcring(s):
        return vring(NC + s, vc, pl.multiple_of(s * FC, FC // 2), FC)

    e1ring = vring(2 * NC, e1, 0, 1024)
    vgring = vring(2 * NC + 1, vg, 0, FFL)
    vuring = vring(2 * NC + 2, vu, 0, FFL)

    def wown(s):
        wring(s).own(w_h.at[pl.ds(pl.multiple_of(s * FC, FC), FC), :])

    other_cols = pl.ds(pl.multiple_of((1 - yh) * KH + z * 512, 512), 512)
    zcol = pl.ds(pl.multiple_of(z * 512, 512), 512)
    dy_cp = [
        remote(dy_h.at[:, other_cols], lhs.at[pl.ds(288, TOK), zcol], y_s.at[0], y_r.at[0], cross),
        remote(vdy_h.at[:, other_cols], lhs.at[pl.ds(544, VAL), zcol], y_s.at[1], y_r.at[1], cross),
    ]
    for cp in dy_cp:
        cp.start()
    e1_cp = [
        remote(vx_h, e1.at[own_rows, pl.ds(0, 512)], y_s.at[2], y_r.at[2], ypart),
        remote(vdy_h.at[:, hid_cols], e1.at[own_rows, pl.ds(512, 512)], y_s.at[3], y_r.at[3], ypart),
    ]
    for cp in e1_cp:
        cp.start()
    wown(0)
    v_cp = [
        remote(vg_h, vg.at[own_rows, :], y_s.at[4], y_r.at[4], ypart),
        remote(vu_h, vu.at[own_rows, :], y_s.at[5], y_r.at[5], ypart),
    ]
    for cp in v_cp:
        cp.start()
    wown(1)
    for cp in local:
        cp.wait()
    cacc[...] = jnp.zeros_like(cacc)
    hacc[...] = jnp.zeros_like(hacc)
    for cp in e1_cp:
        cp.wait_recv()
    e1ring.own()
    wown(2)

    def z_dy(d, zz):
        ref = lhs.at[pl.ds(288, 288), pl.ds(pl.multiple_of(zz * 512, 512), 512)]
        return remote(ref, ref, z_s.at[d - 1], z_r.at[d - 1], zdev[d - 1])

    def z_rs(d):
        to = (z + d) % 4
        return remote(
            iop.at[pl.ds(to * 2, 2)], ior.at[d - 1], z_s.at[2 + d], z_r.at[2 + d], zdev[d - 1]
        )

    def z_ag(d, zz):
        ref = iof.at[pl.ds(zz * 2, 2)]
        return remote(ref, ref, z_s.at[5 + d], z_r.at[5 + d], zdev[d - 1])

    def yl_rs():
        return remote(ios.at[1 - yl], ioy, z_s.at[9], z_r.at[9], ylp)

    def yl_ag(who):
        ref = iof.at[z * 2 + who]
        return remote(ref, ref, z_s.at[10], z_r.at[10], ylp)

    def part_cp(s):
        return remote(psend.at[s], precv.at[s], p_s.at[s], p_r.at[s], ypart)

    def cols(s):
        return pl.ds(pl.multiple_of(s * FC, FC), FC)

    def out_cp(s):
        return [
            pltpu.make_async_copy(gg.at[:, cols(s)], gg_o.at[:, cols(s)], osem.at[0, s]),
            pltpu.make_async_copy(ug.at[:, cols(s)], ug_o.at[:, cols(s)], osem.at[1, s]),
        ]

    def partial_stage(s, carry):
        wring(s).full()
        res = dot_t(lhs[...], wbuf[cols(s), :])
        psend[s, 0:288, :] = res[288:576].astype(BF)
        psend[s, 288:320, :] = res[256:288].astype(BF)
        ownp[s, 0:288, :] = res[0:288]
        ownp[s, 288:320, :] = res[544:576]
        part_cp(s).start()
        return carry

    def grad_stage(s):
        part_cp(s).wait_recv()
        vcot = ownp[s, 256:320, :] + precv[s, 256:320, :].astype(F32)
        base = me_blk * BW
        vc[pl.ds(pl.multiple_of(base + yh * VAL, VAL), VAL), cols(s)] = vcot[0:32].astype(BF)
        vc[pl.ds(pl.multiple_of(base + (1 - yh) * VAL, VAL), VAL), cols(s)] = vcot[32:64].astype(BF)
        cot = ownp[s, 0:256, :] + precv[s, 0:256, :].astype(F32)
        h, g, u = parts(cot, gate[:, cols(s)], up[:, cols(s)])
        hd[:, cols(s)] = h
        gg[:, cols(s)] = g
        ug[:, cols(s)] = u
        vcring(s).own()
        for cp in out_cp(s):
            cp.start()

    def gram_stage(s, carry):
        vcring(s).full()
        h, g, u = parts(vc[:, cols(s)].astype(F32), vg[:, cols(s)], vu[:, cols(s)])
        cacc[...] += dot_t(g, gg[:, cols(s)]) + dot_t(u, ug[:, cols(s)])
        hacc[...] += dot_t(h, hd[:, cols(s)])
        return carry

    def step(i, carry):
        @pl.when(i < NC)
        def _():
            wring(i).forward()

        @pl.when(i < NC - 3)
        def _():
            wown(i + 3)

        @pl.when(i == 0)
        def _():
            for cp in dy_cp:
                cp.wait_recv()
            for d in (1, 2, 3):
                z_dy(d, z).start()
            e1ring.forward()

        @pl.when((i >= 1) & (i < NC + 1))
        def _():
            wring(i - 1).last()

        @pl.when(i == 1)
        def _():
            e1ring.last()

        @pl.when(i == 2)
        def _():
            e1ring.full()
            gi = dot_t(e1[:, 0:512], tx[...])
            go = dot_t(e1[:, 512:1024], tdy[...])
            for p in range(8):
                iop[p, 0] = gi[p * 64 : p * 64 + 64]
                iop[p, 1] = go[p * 64 : p * 64 + 64]
            for d in (1, 2, 3):
                z_rs(d).start()

        @pl.when(i == NC - 1)
        def _():
            for cp in v_cp:
                cp.wait_recv()
            vgring.own()
            vuring.own()

        @pl.when(i == 4)
        def _():
            for d in (1, 2, 3):
                z_dy(d, (z + 4 - d) % 4).wait_recv()

        lo = jnp.clip(jnp.minimum(2 * (i - 4), i - 2), 0, NC)
        hi = jnp.clip(jnp.minimum(2 * (i - 3), i - 1), 0, NC)
        lax.fori_loop(lo, hi, partial_stage, 0)

        @pl.when((i >= 5) & (i < NC + 5))
        def _():
            grad_stage(i - 5)

        @pl.when(i == 5)
        def _():
            for d in (1, 2, 3):
                z_rs(d).wait_recv()
            ios[...] = iop[pl.ds(z * 2, 2)] + ior[0] + ior[1] + ior[2]
            yl_rs().start()

        @pl.when(i == 6)
        def _():
            yl_rs().wait_recv()
            iof[z * 2 + yl] = ios[yl] + ioy[...]
            yl_ag(yl).start()

        @pl.when(i == 7)
        def _():
            yl_ag(1 - yl).wait_recv()
            for d in (1, 2, 3):
                z_ag(d, z).start()

        @pl.when((i >= 6) & (i < NC + 6))
        def _():
            vcring(i - 6).forward()

        @pl.when((i >= 7) & (i < NC + 7))
        def _():
            vcring(i - 7).last()

        @pl.when(i == 8)
        def _():
            vgring.forward()

        @pl.when(i == 9)
        def _():
            vuring.forward()
            vgring.last()

        @pl.when(i == 10)
        def _():
            vuring.last()
            vgring.full()
            vuring.full()

        glo = jnp.where(i <= 10, 0, i - 8)
        ghi = jnp.where(i < 10, 0, i - 7)
        lax.fori_loop(glo, ghi, gram_stage, 0)
        return carry

    lax.fori_loop(0, NC + 8, step, 0)

    for d in (1, 2, 3):
        z_ag(d, (z + 4 - d) % 4).wait_recv()
    sums = []
    for v in (0, 1):
        acc = jnp.zeros((VAL, TOK), F32)
        for p in range(8):
            r = slice(p * 64 + v * VAL, p * 64 + v * VAL + VAL)
            q = slice(v * VAL, v * VAL + VAL)
            acc += iof[p, 0, q, :] * cacc[r, :] + iof[p, 1, q, :] * hacc[r, :]
        acc = acc[:, 0:128] + acc[:, 128:256]
        sums.append(acc[0:8] + acc[8:16] + acc[16:24] + acc[24:32])
    for v in (0, 1):
        fin_s[v * 8 : v * 8 + 8, :] = sums[v]
    fin = [remote(fin_s, fin_r.at[n], f_s.at[n], f_r.at[n], to) for n, to in enumerate(hids)]
    for cp in fin:
        cp.start()
    for cp in dy_cp + e1_cp + v_cp:
        cp.wait_send()
    for d in (1, 2, 3):
        z_dy(d, z).wait_send()
        z_rs(d).wait_send()
        z_ag(d, z).wait_send()
    yl_rs().wait_send()
    yl_ag(yl).wait_send()
    e1ring.drain()
    vgring.drain()
    vuring.drain()

    def drain(s, carry):
        wring(s).drain()
        vcring(s).drain()
        part_cp(s).wait_send()
        for cp in out_cp(s):
            cp.wait()
        return carry

    lax.fori_loop(0, NC, drain, 0)
    for cp in fin:
        cp.wait()
    total = fin_s[...]
    for n in range(7):
        total = total + fin_r[n]
    scale = -step_rate / (LEN * LEN)
    s0 = jnp.sum(total[0:8]) * scale
    s1 = jnp.sum(total[8:16]) * scale
    lane = lax.broadcasted_iota(jnp.int32, (1, 2), 1)
    sc_o[...] = jnp.where(lane == 0, s0, s1)


def per_device(*args):
    vm = pltpu.VMEM
    dma = pltpu.SemaphoreType.DMA
    hbm = pl.BlockSpec(memory_space=pl.ANY)
    return pl.pallas_call(
        kernel,
        out_shape=(
            jax.ShapeDtypeStruct((TOK, FFL), BF),
            jax.ShapeDtypeStruct((TOK, FFL), BF),
            jax.ShapeDtypeStruct((1, 2), F32),
        ),
        in_specs=[hbm] * 9,
        out_specs=(hbm, hbm, pl.BlockSpec(memory_space=pltpu.VMEM)),
        scratch_shapes=[
            vm((FFL, KH), BF),
            vm((576, KH), BF),
            vm((TOK, 512), BF),
            vm((TOK, 512), BF),
            vm((TOK, FFL), BF),
            vm((TOK, FFL), BF),
            vm((512, 1024), BF),
            vm((512, FFL), BF),
            vm((512, FFL), BF),
            vm((512, FFL), BF),
            vm((NC, 320, FC), F32),
            vm((NC, 320, FC), BF),
            vm((NC, 320, FC), BF),
            vm((TOK, FFL), BF),
            vm((TOK, FFL), BF),
            vm((TOK, FFL), BF),
            vm((8, 2, 64, TOK), F32),
            vm((3, 2, 2, 64, TOK), F32),
            vm((2, 2, 64, TOK), F32),
            vm((2, 64, TOK), F32),
            vm((8, 2, 64, TOK), F32),
            vm((512, TOK), F32),
            vm((512, TOK), F32),
            vm((16, 128), F32),
            vm((7, 16, 128), F32),
            dma((11,)),
            dma((2, NC)),
            dma((2 * NC + 3, 8)),
            dma((2 * NC + 3, 8)),
            dma((6,)),
            dma((6,)),
            dma((NC,)),
            dma((NC,)),
            dma((11,)),
            dma((11,)),
            dma((7,)),
            dma((7,)),
        ],
        compiler_params=pltpu.CompilerParams(
            collective_id=0, has_side_effects=True, vmem_limit_bytes=56 * 1024 * 1024
        ),
    )(*args)


def solution(mesh):
    return jax.shard_map(
        per_device,
        mesh=mesh,
        in_specs=(
            P("dp", "hid"),
            P("dp", "hid"),
            P("dp", "hid"),
            P("dp", None),
            P("dp", "hid"),
            P("dp", "hid"),
            P("dp", "hid"),
            P("dp", None),
            P("hid", "dp"),
        ),
        out_specs=(P("dp", "hid"), P("dp", "hid"), P("dp", None)),
        check_vma=False,
    )
```

```python
import functools

import jax
import jax.numpy as jnp
from jax import lax
from jax.experimental import pallas as pl
from jax.experimental.pallas import tpu as pltpu
from jax.sharding import PartitionSpec as P

LEN = 256
step_rate = 0.1
MESH = pl.DeviceIdType.MESH
scope = jax.named_scope
BF = jnp.bfloat16
F32 = jnp.float32

TOK = 256
VAL = 32
FFL = 1792
FC = 256
NC = FFL // FC
KH = 2048
BW = 64


def dot_t(a, b):
    return lax.dot_general(a, b, (((1,), (1,)), ((), ())), preferred_element_type=F32)


def parts(cot, gate, up):
    a = gate.astype(F32)
    b = up.astype(F32)
    s = jax.nn.sigmoid(a)
    silu = a * s
    hidden = (silu * b).astype(BF)
    gate_grad = (cot * b * s * (1.0 + a * (1.0 - s))).astype(BF)
    up_grad = (cot * silu).astype(BF)
    return hidden, gate_grad, up_grad


def kernel(
    tx_h, gate_h, up_h, dy_h, vx_h, vg_h, vu_h, vdy_h, w_h,
    gg, ug, sc_o,
    wbuf, lhs, tx, tdy, gate, up, e1, vg, vu, vc, ownp, psend, precv, hd,
    iop, ior, ios, ioy, iof, cacc, hacc, fin_s, fin_r,
    lsem, ring_s, ring_r, e_s, e_r, y_s, y_r, p_s, p_r, z_s, z_r, f_s, f_r,
):
    i_dp = lax.axis_index("dp")
    i_hid = lax.axis_index("hid")
    yh, x, k = i_dp // 8, (i_dp // 2) % 4, i_dp % 2
    yl, z = i_hid // 4, i_hid % 4
    xm, xp, x2 = (x + 3) % 4, (x + 1) % 4, (x + 2) % 4

    def dev(yh_=yh, x_=x, k_=k, yl_=yl, z_=z):
        return ((yh_ * 4 + x_) * 2 + k_, yl_ * 4 + z_)

    right, left, sib = dev(x_=xp), dev(x_=xm), dev(k_=1 - k)
    ypart, cross, ylp = dev(yh_=1 - yh), dev(yh_=1 - yh, yl_=1 - yl), dev(yl_=1 - yl)
    zdev = [dev(z_=(z + d) % 4) for d in (1, 2, 3)]
    hids = zdev + [dev(yl_=1 - yl, z_=(z + d) % 4) for d in range(4)]

    def remote(src, dst, ss, rs, to):
        return pltpu.make_async_remote_copy(
            src_ref=src, dst_ref=dst, send_sem=ss, recv_sem=rs, device_id=to, device_id_type=MESH
        )

    me_blk = x * 2 + k
    own_rows = pl.ds(pl.multiple_of(me_blk * BW + yh * VAL, VAL), VAL)
    half_cols = pl.ds(pl.multiple_of(yh * KH, KH), KH)
    hid_cols = pl.ds(pl.multiple_of(i_hid * 512, 512), 512)
    wcol = pl.ds(pl.multiple_of(me_blk * 256, 256), 256)
    local = [
        (w_h, wbuf.at[:, wcol]),
        (vx_h, e1.at[own_rows, pl.ds(0, 512)]),
        (vdy_h.at[:, hid_cols], e1.at[own_rows, pl.ds(512, 512)]),
        (vg_h, vg.at[own_rows, :]),
        (vu_h, vu.at[own_rows, :]),
        (dy_h.at[:, half_cols], lhs.at[pl.ds(0, TOK), :]),
        (vdy_h.at[:, half_cols], lhs.at[pl.ds(TOK, VAL), :]),
        (tx_h, tx),
        (dy_h.at[:, hid_cols], tdy),
        (gate_h, gate),
        (up_h, up),
    ]
    local = [pltpu.make_async_copy(a, b, lsem.at[n]) for n, (a, b) in enumerate(local)]
    for cp in local:
        cp.start()

    barrier = pltpu.get_barrier_semaphore()
    greet = [right, left, dev(x_=x2), sib, ypart, cross] + hids
    for to in greet:
        pl.semaphore_signal(barrier, inc=1, device_id=to, device_id_type=MESH)
    with scope("barrier"):
        pl.semaphore_wait(barrier, len(greet))

    class Ring:
        def __init__(self, slot, view, half):
            self.slot, self.view, self.half = slot, view, half

        def cp(self, n, ref, to):
            return remote(ref, ref, ring_s.at[self.slot, n], ring_r.at[self.slot, n], to)

        def own(self, src=None):
            for n, to in ((0, right), (1, left), (4, sib)):
                ref = self.view(x, k)
                remote(
                    ref if src is None else src, ref,
                    ring_s.at[self.slot, n], ring_r.at[self.slot, n], to,
                ).start()

        def forward(self):
            self.cp(0, self.view(xm, k), right).wait_recv()
            self.cp(2, self.half(xm, k, 0), right).start()
            self.cp(5, self.view(xm, k), sib).start()
            self.cp(1, self.view(xp, k), left).wait_recv()
            self.cp(3, self.half(xp, k, 1), left).start()
            self.cp(6, self.view(xp, k), sib).start()

        def last(self):
            self.cp(2, self.half(x2, k, 0), right).wait_recv()
            self.cp(3, self.half(x2, k, 1), left).wait_recv()
            self.cp(7, self.view(x2, k), sib).start()

        def full(self):
            for n, xx in ((4, x), (5, xm), (6, xp), (7, x2)):
                self.cp(n, self.view(xx, 1 - k), sib).wait_recv()

        def drain(self):
            for n in (0, 1, 4, 5, 6, 7):
                self.cp(n, self.view(x, k), sib).wait_send()
            for n in (2, 3):
                self.cp(n, self.half(x, k, 0), sib).wait_send()

    def wring(s):
        def view(xx, kk):
            return wbuf.at[
                pl.ds(pl.multiple_of(s * FC, FC), FC),
                pl.ds(pl.multiple_of((xx * 2 + kk) * 256, 256), 256),
            ]

        def half(xx, kk, n):
            return wbuf.at[
                pl.ds(pl.multiple_of(s * FC + n * (FC // 2), FC // 2), FC // 2),
                pl.ds(pl.multiple_of((xx * 2 + kk) * 256, 256), 256),
            ]

        return Ring(s, view, half)

    def vring(slot, buf, first, width):
        def rows(xx, kk):
            return pl.ds(pl.multiple_of((xx * 2 + kk) * BW, BW), BW)

        def view(xx, kk):
            return buf.at[rows(xx, kk), pl.ds(first, width)]

        def half(xx, kk, n):
            return buf.at[rows(xx, kk), pl.ds(first + n * (width // 2), width // 2)]

        return Ring(slot, view, half)

    def vcring(s):
        return vring(NC + s, vc, pl.multiple_of(s * FC, FC // 2), FC)

    vgring = vring(2 * NC, vg, 0, FFL)
    vuring = vring(2 * NC + 1, vu, 0, FFL)

    def wown(s):
        wring(s).own(w_h.at[pl.ds(pl.multiple_of(s * FC, FC), FC), :])

    other_cols = pl.ds(pl.multiple_of((1 - yh) * KH + z * 512, 512), 512)
    zcol = pl.ds(pl.multiple_of(z * 512, 512), 512)

    def yh_cp(n, src, dst, to):
        return remote(src, dst, y_s.at[n], y_r.at[n], to)

    def e1_blk(xx, kk, half_, n):
        rows = pl.multiple_of((xx * 2 + kk) * BW + half_ * VAL, VAL)
        return e1.at[pl.ds(rows, n), :]

    xdev = (right, left, dev(x_=x2))
    xsrc = (xm, xp, x2)

    def e1_x(d, n):
        src = vx_h if n == 0 else vdy_h.at[:, hid_cols]
        return remote(
            src, e1.at[own_rows, pl.ds(n * 512, 512)], e_s.at[d, n], e_r.at[d, n], xdev[d]
        )

    e1_cp = [e1_x(d, n) for d in range(3) for n in range(2)]

    def e1_y(n, who):
        xx = (x, xm, xp, x2)[n]
        ref = e1_blk(xx, k, who, VAL)
        return remote(ref, ref, e_s.at[3 + n, 0], e_r.at[3 + n, 0], ypart)

    def e1_sib(n, kk):
        xx = (x, xm, xp, x2)[n]
        ref = e1_blk(xx, kk, 0, BW)
        return remote(ref, ref, e_s.at[3 + n, 1], e_r.at[3 + n, 1], sib)

    lo_rows, hi_rows = pl.ds(0, 128), pl.ds(128, 128)
    dy_cp = [
        yh_cp(0, dy_h.at[lo_rows, other_cols], lhs.at[pl.ds(288, 128), zcol], cross),
        yh_cp(1, dy_h.at[hi_rows, other_cols], lhs.at[pl.ds(416, 128), zcol], cross),
        yh_cp(6, vdy_h.at[:, other_cols], lhs.at[pl.ds(544, VAL), zcol], cross),
    ]
    v_cp = [
        yh_cp(4, vg_h, vg.at[own_rows, :], ypart),
        yh_cp(5, vu_h, vu.at[own_rows, :], ypart),
    ]
    for cp in dy_cp + e1_cp:
        cp.start()
    for c in range(4):
        wown(c)

    def z_dy(n, d, zz):
        ref = lhs.at[
            pl.ds(288 + n * 128, 128 + n * 32), pl.ds(pl.multiple_of(zz * 512, 512), 512)
        ]
        return remote(ref, ref, z_s.at[n, d - 1], z_r.at[n, d - 1], zdev[d - 1])

    def z_rs(d):
        to = (z + d) % 4
        return remote(
            iop.at[pl.ds(to * 2, 2)], ior.at[d - 1], z_s.at[2, d - 1], z_r.at[2, d - 1], zdev[d - 1]
        )

    def z_ag(d, zz):
        ref = iof.at[pl.ds(zz * 2, 2)]
        return remote(ref, ref, z_s.at[3, d - 1], z_r.at[3, d - 1], zdev[d - 1])

    def yl_rs():
        return remote(ios.at[1 - yl], ioy, z_s.at[4, 0], z_r.at[4, 0], ylp)

    def yl_ag(who):
        ref = iof.at[z * 2 + who]
        return remote(ref, ref, z_s.at[4, 1], z_r.at[4, 1], ylp)

    def part_cp(s):
        return remote(psend.at[s], precv.at[s], p_s.at[s], p_r.at[s], ypart)

    def cols(s):
        return pl.ds(pl.multiple_of(s * FC, FC), FC)

    def partial_stage(s, carry):
        with scope("wfull"):
            wring(s).full()
        res = dot_t(lhs[...], wbuf[cols(s), :])
        psend[s, 0:288, :] = res[288:576].astype(BF)
        psend[s, 288:320, :] = res[256:288].astype(BF)
        ownp[s, 0:288, :] = res[0:288]
        ownp[s, 288:320, :] = res[544:576]
        part_cp(s).start()
        return carry

    def grad_stage(s):
        with scope("gradwait"):
            part_cp(s).wait_recv()
        vcot = ownp[s, 256:320, :] + precv[s, 256:320, :].astype(F32)
        base = me_blk * BW
        vc[pl.ds(pl.multiple_of(base + yh * VAL, VAL), VAL), cols(s)] = vcot[0:32].astype(BF)
        vc[pl.ds(pl.multiple_of(base + (1 - yh) * VAL, VAL), VAL), cols(s)] = vcot[32:64].astype(BF)
        cot = ownp[s, 0:256, :] + precv[s, 0:256, :].astype(F32)
        h, g, u = parts(cot, gate[:, cols(s)], up[:, cols(s)])
        hd[:, cols(s)] = h
        gg[:, cols(s)] = g
        ug[:, cols(s)] = u
        vcring(s).own()

    def gram_stage(s, carry):
        vcring(s).full()
        h, g, u = parts(vc[:, cols(s)].astype(F32), vg[:, cols(s)], vu[:, cols(s)])
        cacc[...] += dot_t(g, gg[:, cols(s)]) + dot_t(u, ug[:, cols(s)])
        hacc[...] += dot_t(h, hd[:, cols(s)])
        return carry

    cacc[...] = jnp.zeros_like(cacc)
    hacc[...] = jnp.zeros_like(hacc)
    with scope("dyA"):
        dy_cp[0].wait_recv()
        for d in (1, 2, 3):
            z_dy(0, d, z).start()

    def step(i, carry):
        @pl.when(i < NC)
        def _():
            with scope("wfwd"):
                wring(i).forward()

        @pl.when(i < NC - 4)
        def _():
            wown(i + 4)

        @pl.when(i == 0)
        def _():
            with scope("dyB"):
                dy_cp[1].wait_recv()
                dy_cp[2].wait_recv()
                for d in (1, 2, 3):
                    z_dy(1, d, z).start()
            with scope("e1x"):
                for n in (1, 2):
                    local[n].wait()
                for cp in e1_cp:
                    cp.wait_recv()
                for n in range(4):
                    e1_y(n, yh).start()
                for cp in v_cp:
                    cp.start()

        @pl.when(i == 2)
        def _():
            with scope("e1y"):
                for n in range(4):
                    e1_y(n, 1 - yh).wait_recv()
                for n in range(4):
                    e1_sib(n, k).start()

        @pl.when((i >= 3) & (i < NC + 3))
        def _():
            with scope("wlast"):
                wring(i - 3).last()

        @pl.when(i == 3)
        def _():
            with scope("e1full"):
                for n in range(4):
                    e1_sib(n, 1 - k).wait_recv()
                local[7].wait()
                local[8].wait()
            with scope("iogram"):
                gi = dot_t(e1[:, 0:512], tx[...])
                go = dot_t(e1[:, 512:1024], tdy[...])
                for p in range(8):
                    iop[p, 0] = gi[p * 64 : p * 64 + 64]
                    iop[p, 1] = go[p * 64 : p * 64 + 64]
                for d in (1, 2, 3):
                    z_rs(d).start()

        @pl.when(i == NC - 1)
        def _():
            with scope("vown"):
                for cp in v_cp:
                    cp.wait_recv()
                local[3].wait()
                local[4].wait()
                vgring.own()
                vuring.own()

        @pl.when(i == 4)
        def _():
            with scope("zdy"):
                for n in (0, 5, 6):
                    local[n].wait()
                for n in (0, 1):
                    for d in (1, 2, 3):
                        z_dy(n, d, (z + 4 - d) % 4).wait_recv()

        with scope("part"):
            lo = jnp.where(i == 4, 0, i - 3)
            hi = jnp.where((i >= 4) & (i < NC + 3), i - 2, lo)
            lax.fori_loop(lo, hi, partial_stage, 0)

        @pl.when(i == 10)
        def _():
            with scope("vgfwd"):
                vgring.forward()

        @pl.when(i == NC + 5)
        def _():
            with scope("vufwd"):
                vuring.forward()

        @pl.when(i == 7)
        def _():
            with scope("iors"):
                for d in (1, 2, 3):
                    z_rs(d).wait_recv()
                ios[...] = iop[pl.ds(z * 2, 2)] + ior[0] + ior[1] + ior[2]
                yl_rs().start()

        @pl.when(i == 5)
        def _():
            for n in (9, 10):
                local[n].wait()

        @pl.when((i >= 7) & (i < NC + 7))
        def _():
            with scope("grad"):
                grad_stage(i - 7)

        @pl.when(i == 11)
        def _():
            with scope("ylrs"):
                yl_rs().wait_recv()
                iof[z * 2 + yl] = (ios[yl] + ioy[...]).astype(BF)
                yl_ag(yl).start()

        @pl.when(i == NC + 6)
        def _():
            with scope("ylag"):
                yl_ag(1 - yl).wait_recv()
                for d in (1, 2, 3):
                    z_ag(d, z).start()

        return carry

    lax.fori_loop(0, NC + 7, step, 0)
    def vc_forward(m, carry):
        vcring(m).forward()
        return carry

    def vc_last(m, carry):
        vcring(m).last()
        return carry

    with scope("vcfwd"):
        lax.fori_loop(0, NC, vc_forward, 0)
    with scope("vglast"):
        vgring.last()
    with scope("vulast"):
        vuring.last()
    with scope("vclast"):
        lax.fori_loop(0, NC, vc_last, 0)
    with scope("vfull"):
        vgring.full()
        vuring.full()
    with scope("gram"):
        lax.fori_loop(0, NC, gram_stage, 0)

    with scope("zag"):
        for d in (1, 2, 3):
            z_ag(d, (z + 4 - d) % 4).wait_recv()
    sums = []
    for v in (0, 1):
        acc = jnp.zeros((VAL, TOK), F32)
        for p in range(8):
            r = slice(p * 64 + v * VAL, p * 64 + v * VAL + VAL)
            q = slice(v * VAL, v * VAL + VAL)
            acc += iof[p, 0, q, :].astype(F32) * cacc[r, :] + iof[p, 1, q, :].astype(F32) * hacc[r, :]
        acc = acc[:, 0:128] + acc[:, 128:256]
        sums.append(acc[0:8] + acc[8:16] + acc[16:24] + acc[24:32])
    for v in (0, 1):
        fin_s[v * 8 : v * 8 + 8, :] = sums[v]
    fin = [remote(fin_s, fin_r.at[n], f_s.at[n], f_r.at[n], to) for n, to in enumerate(hids)]
    for cp in fin:
        cp.start()
    for cp in dy_cp + e1_cp + v_cp:
        cp.wait_send()
    for d in (1, 2, 3):
        z_dy(0, d, z).wait_send()
        z_dy(1, d, z).wait_send()
        z_rs(d).wait_send()
        z_ag(d, z).wait_send()
    yl_rs().wait_send()
    yl_ag(yl).wait_send()
    for n in range(4):
        e1_y(n, yh).wait_send()
        e1_sib(n, k).wait_send()
    vgring.drain()
    vuring.drain()

    def drain(s, carry):
        wring(s).drain()
        vcring(s).drain()
        part_cp(s).wait_send()
        return carry

    lax.fori_loop(0, NC, drain, 0)
    with scope("finwait"):
        for cp in fin:
            cp.wait()
    total = fin_s[...]
    for n in range(7):
        total = total + fin_r[n]
    scale = -step_rate / (LEN * LEN)
    s0 = jnp.sum(total[0:8]) * scale
    s1 = jnp.sum(total[8:16]) * scale
    lane = lax.broadcasted_iota(jnp.int32, (1, 2), 1)
    sc_o[...] = jnp.where(lane == 0, s0, s1)


def per_device(*args):
    vm = pltpu.VMEM
    dma = pltpu.SemaphoreType.DMA
    hbm = pl.BlockSpec(memory_space=pl.ANY)
    vmem = pl.BlockSpec(memory_space=pltpu.VMEM)
    return pl.pallas_call(
        kernel,
        out_shape=(vm((TOK, FFL), BF), vm((TOK, FFL), BF), vm((1, 2), F32)),
        in_specs=[hbm] * 9,
        out_specs=(vmem, vmem, vmem),
        scratch_shapes=[
            vm((FFL, KH), BF),
            vm((576, KH), BF),
            vm((TOK, 512), BF),
            vm((TOK, 512), BF),
            vm((TOK, FFL), BF),
            vm((TOK, FFL), BF),
            vm((512, 1024), BF),
            vm((512, FFL), BF),
            vm((512, FFL), BF),
            vm((512, FFL), BF),
            vm((NC, 320, FC), F32),
            vm((NC, 320, FC), BF),
            vm((NC, 320, FC), BF),
            vm((TOK, FFL), BF),
            vm((8, 2, 64, TOK), F32),
            vm((3, 2, 2, 64, TOK), F32),
            vm((2, 2, 64, TOK), F32),
            vm((2, 64, TOK), F32),
            vm((8, 2, 64, TOK), BF),
            vm((512, TOK), F32),
            vm((512, TOK), F32),
            vm((16, 128), F32),
            vm((7, 16, 128), F32),
            dma((11,)),
            dma((2 * NC + 2, 8)),
            dma((2 * NC + 2, 8)),
            dma((7, 2)),
            dma((7, 2)),
            dma((7,)),
            dma((7,)),
            dma((NC,)),
            dma((NC,)),
            dma((5, 3)),
            dma((5, 3)),
            dma((7,)),
            dma((7,)),
        ],
        compiler_params=pltpu.CompilerParams(
            collective_id=0, has_side_effects=True, vmem_limit_bytes=56 * 1024 * 1024
        ),
    )(*args)


def solution(mesh):
    return jax.shard_map(
        per_device,
        mesh=mesh,
        in_specs=(
            P("dp", "hid"),
            P("dp", "hid"),
            P("dp", "hid"),
            P("dp", None),
            P("dp", "hid"),
            P("dp", "hid"),
            P("dp", "hid"),
            P("dp", None),
            P("hid", "dp"),
        ),
        out_specs=(P("dp", "hid"), P("dp", "hid"), P("dp", None)),
        check_vma=False,
    )
```

```python
import functools

import jax
import jax.numpy as jnp
from jax import lax
from jax.experimental import pallas as pl
from jax.experimental.pallas import tpu as pltpu
from jax.sharding import PartitionSpec as P

LEN = 256
step_rate = 0.1
MESH = pl.DeviceIdType.MESH
scope = jax.named_scope
BF = jnp.bfloat16
F32 = jnp.float32

TOK = 256
VAL = 32
FFL = 1792
FC = 256
NC = FFL // FC
KH = 2048
PIECES = 4
LEAD = 3
VA, VB = 8 * FC, 6 * FC
BW = 64


def dot_t(a, b):
    return lax.dot_general(a, b, (((1,), (1,)), ((), ())), preferred_element_type=F32)


def parts(cot, gate, up):
    a = gate.astype(F32)
    b = up.astype(F32)
    s = jax.nn.sigmoid(a)
    silu = a * s
    hidden = (silu * b).astype(BF)
    gate_grad = (cot * b * s * (1.0 + a * (1.0 - s))).astype(BF)
    up_grad = (cot * silu).astype(BF)
    return hidden, gate_grad, up_grad


def kernel(
    tx_h, gate_h, up_h, dy_h, vx_h, vg_h, vu_h, vdy_h, w_h,
    gg, ug, total_o,
    wbuf, lhs, tx, tdy, gate, up, e1, vv, vc, ownp, psend, precv, hd,
    iop, ior, ios, iosb, ioy, iof, cacc, hacc, fin_s, fin_r,
    lsem, ring_s, ring_r, e_s, e_r, y_s, y_r, p_s, p_r, z_s, z_r, f_s, f_r,
):
    i_dp = lax.axis_index("dp")
    i_hid = lax.axis_index("hid")
    yh, x, k = i_dp // 8, (i_dp // 2) % 4, i_dp % 2
    yl, z = i_hid // 4, i_hid % 4
    xm, xp, x2 = (x + 3) % 4, (x + 1) % 4, (x + 2) % 4

    def dev(yh_=yh, x_=x, k_=k, yl_=yl, z_=z):
        return ((yh_ * 4 + x_) * 2 + k_, yl_ * 4 + z_)

    right, left, sib = dev(x_=xp), dev(x_=xm), dev(k_=1 - k)
    ypart, cross, ylp = dev(yh_=1 - yh), dev(yh_=1 - yh, yl_=1 - yl), dev(yl_=1 - yl)
    zdev = [dev(z_=(z + d) % 4) for d in (1, 2, 3)]
    hids = zdev + [dev(yl_=1 - yl, z_=(z + d) % 4) for d in range(4)]

    def remote(src, dst, ss, rs, to):
        return pltpu.make_async_remote_copy(
            src_ref=src, dst_ref=dst, send_sem=ss, recv_sem=rs, device_id=to, device_id_type=MESH
        )

    me_blk = x * 2 + k
    own_rows = pl.ds(pl.multiple_of(me_blk * BW + yh * VAL, VAL), VAL)
    half_cols = pl.ds(pl.multiple_of(yh * KH, KH), KH)
    hid_cols = pl.ds(pl.multiple_of(i_hid * 512, 512), 512)
    wcol = pl.ds(pl.multiple_of(me_blk * 256, 256), 256)
    local = [
        (0, w_h, wbuf.at[:, wcol]),
        (1, vx_h, e1.at[own_rows, pl.ds(0, 512)]),
        (1, vdy_h.at[:, hid_cols], e1.at[own_rows, pl.ds(512, 512)]),
        (2, dy_h.at[:, half_cols], lhs.at[pl.ds(0, TOK), :]),
        (2, vdy_h.at[:, half_cols], lhs.at[pl.ds(TOK, VAL), :]),
        (3, tx_h, tx),
        (3, dy_h.at[:, hid_cols], tdy),
        (4, gate_h, gate),
        (4, up_h, up),
    ]
    for c in range(NC):
        for n, src in enumerate((vg_h, vu_h)):
            at = pl.ds((2 * c + n) * FC, FC)
            local.append((5, src.at[:, pl.ds(c * FC, FC)], vv.at[own_rows, at]))
    for n, src, dst in local:
        pltpu.make_async_copy(src, dst, lsem.at[n]).start()

    def take(ref, sem):
        pltpu.make_async_copy(ref, ref, sem).wait()

    local_bytes = (
        wbuf.at[:, pl.ds(0, 256)],
        e1.at[pl.ds(0, VAL), :],
        lhs.at[pl.ds(0, TOK + VAL), :],
        lhs.at[pl.ds(0, 128), :],
        vc,
        vv.at[pl.ds(0, VAL), :],
    )

    def local_wait(n):
        take(local_bytes[n], lsem.at[n])

    barrier = pltpu.get_barrier_semaphore()
    greet = [right, left, dev(x_=x2), sib, ypart, cross] + hids
    for to in greet:
        pl.semaphore_signal(barrier, inc=1, device_id=to, device_id_type=MESH)
    with scope("barrier"):
        pl.semaphore_wait(barrier, len(greet))

    class Ring:
        def __init__(self, kind, slot, view, half, size):
            self.kind, self.slot, self.view, self.half, self.size = kind, slot, view, half, size

        def send(self, n, ref, to, src=None):
            remote(
                ref if src is None else src, ref, ring_s.at[self.kind], ring_r.at[self.slot, n], to
            ).start()

        def own(self, src=None):
            for n, to in ((0, right), (0, left), (2, sib)):
                self.send(n, self.view(x, k), to, src)

        def forward(self):
            take(self.size(2), ring_r.at[self.slot, 0])
            self.send(1, self.half(xm, k, 0), right)
            self.send(1, self.half(xp, k, 1), left)
            self.send(2, self.view(xm, k), sib)
            self.send(2, self.view(xp, k), sib)

        def last(self):
            take(self.size(1), ring_r.at[self.slot, 1])
            self.send(2, self.view(x2, k), sib)

        def full(self):
            take(self.size(4), ring_r.at[self.slot, 2])

    def wring(s):
        def view(xx, kk):
            return wbuf.at[
                pl.ds(pl.multiple_of(s * FC, FC), FC),
                pl.ds(pl.multiple_of((xx * 2 + kk) * 256, 256), 256),
            ]

        def half(xx, kk, n):
            return wbuf.at[
                pl.ds(pl.multiple_of(s * FC + n * (FC // 2), FC // 2), FC // 2),
                pl.ds(pl.multiple_of((xx * 2 + kk) * 256, 256), 256),
            ]

        def size(n):
            return wbuf.at[pl.ds(0, n * FC), pl.ds(0, 256)]

        return Ring(0, s, view, half, size)

    def vring(kind, slot, buf, first, width):
        def rows(xx, kk):
            return pl.ds(pl.multiple_of((xx * 2 + kk) * BW, BW), BW)

        def view(xx, kk):
            return buf.at[rows(xx, kk), pl.ds(first, width)]

        def half(xx, kk, n):
            return buf.at[rows(xx, kk), pl.ds(first + n * (width // 2), width // 2)]

        def size(n):
            return buf.at[pl.ds(0, n * BW), pl.ds(0, width)]

        return Ring(kind, slot, view, half, size)

    def vcring(s):
        return vring(1, NC + s, vc, pl.multiple_of(s * FC, FC // 2), FC)

    varing = vring(2, 2 * NC, vv, 0, VA)
    vbring = vring(2, 2 * NC + 1, vv, VA, VB)

    def wown(s):
        wring(s).own(w_h.at[pl.ds(pl.multiple_of(s * FC, FC), FC), :])

    other_cols = pl.ds(pl.multiple_of((1 - yh) * KH + z * 512, 512), 512)
    zcol = pl.ds(pl.multiple_of(z * 512, 512), 512)

    def yh_cp(n, src, dst, to):
        return remote(src, dst, y_s.at[n // 2], y_r.at[n], to)

    def e1_blk(xx, kk, half_, n):
        rows = pl.multiple_of((xx * 2 + kk) * BW + half_ * VAL, VAL)
        return e1.at[pl.ds(rows, n), :]

    xdev = (right, left, dev(x_=x2))
    xsrc = (xm, xp, x2)

    def e1_x(d, n):
        src = vx_h if n == 0 else vdy_h.at[:, hid_cols]
        return remote(
            src, e1.at[own_rows, pl.ds(n * 512, 512)], e_s, e_r.at[0], xdev[d]
        )

    e1_cp = [e1_x(d, n) for d in range(3) for n in range(2)]

    def e1_y(n, who):
        xx = (x, xm, xp, x2)[n]
        ref = e1_blk(xx, k, who, VAL)
        return remote(ref, ref, e_s, e_r.at[1], ypart)

    def e1_sib(n, kk):
        xx = (x, xm, xp, x2)[n]
        ref = e1_blk(xx, kk, 0, BW)
        return remote(ref, ref, e_s, e_r.at[2], sib)

    lo_rows, hi_rows = pl.ds(0, 128), pl.ds(128, 128)
    dy_cp = [
        yh_cp(0, dy_h.at[lo_rows, other_cols], lhs.at[pl.ds(288, 128), zcol], cross),
        yh_cp(1, dy_h.at[hi_rows, other_cols], lhs.at[pl.ds(416, 128), zcol], cross),
        yh_cp(1, vdy_h.at[:, other_cols], lhs.at[pl.ds(544, VAL), zcol], cross),
    ]
    v_cp = [
        yh_cp(2, vv.at[own_rows, pl.ds(0, VA)], vv.at[own_rows, pl.ds(0, VA)], ypart),
        yh_cp(2, vv.at[own_rows, pl.ds(VA, VB)], vv.at[own_rows, pl.ds(VA, VB)], ypart),
    ]
    for cp in dy_cp + e1_cp:
        cp.start()
    for c in range(LEAD):
        wown(c)

    def z_dy(n, d, zz):
        ref = lhs.at[
            pl.ds(288 + n * 128, 128 + n * 32), pl.ds(pl.multiple_of(zz * 512, 512), 512)
        ]
        return remote(ref, ref, z_s.at[0], z_r.at[0], zdev[d - 1])

    def z_rs(d):
        to = (z + d) % 4
        return remote(
            iop.at[pl.ds(to * 2, 2)], ior.at[d - 1], z_s.at[1], z_r.at[1], zdev[d - 1]
        )

    def z_ag(d, zz):
        ref = iof.at[pl.ds(zz * 2, 2)]
        return remote(ref, ref, z_s.at[2], z_r.at[2], zdev[d - 1])

    def yl_rs():
        return remote(iosb, ioy, z_s.at[3], z_r.at[3], ylp)

    def yl_ag(who):
        ref = iof.at[z * 2 + who]
        return remote(ref, ref, z_s.at[4], z_r.at[4], ylp)

    def part_cp(s):
        return remote(psend.at[s], precv.at[s], p_s, p_r.at[s], ypart)

    def cols(s):
        return pl.ds(pl.multiple_of(s * FC, FC), FC)

    def partial_stage(s):
        with scope("wfull"):
            wring(s).full()
        res = dot_t(lhs[...], wbuf[cols(s), :])
        psend[s, 0:288, :] = res[288:576].astype(BF)
        psend[s, 288:320, :] = res[256:288].astype(BF)
        ownp[s, 0:288, :] = res[0:288]
        ownp[s, 288:320, :] = res[544:576]
        part_cp(s).start()

    def grad_stage(s):
        with scope("gradwait"):
            part_cp(s).wait_recv()
        vcot = ownp[s, 256:320, :] + precv[s, 256:320, :].astype(F32)
        base = me_blk * BW
        vc[pl.ds(pl.multiple_of(base + yh * VAL, VAL), VAL), cols(s)] = vcot[0:32].astype(BF)
        vc[pl.ds(pl.multiple_of(base + (1 - yh) * VAL, VAL), VAL), cols(s)] = vcot[32:64].astype(BF)
        cot = ownp[s, 0:256, :] + precv[s, 0:256, :].astype(F32)
        h, g, u = parts(cot, gate[:, cols(s)], up[:, cols(s)])
        hd[:, cols(s)] = h
        gg[:, cols(s)] = g
        ug[:, cols(s)] = u
        vcring(s).own()

    def gram_stage(s):
        vcring(s).full()
        g_at, u_at = pl.multiple_of(s * 2 * FC, FC), pl.multiple_of(s * 2 * FC + FC, FC)
        h, g, u = parts(
            vc[:, cols(s)].astype(F32), vv[:, pl.ds(g_at, FC)], vv[:, pl.ds(u_at, FC)]
        )
        cacc[...] += dot_t(g, gg[:, cols(s)]) + dot_t(u, ug[:, cols(s)])
        hacc[...] += dot_t(h, hd[:, cols(s)])

    cacc[...] = jnp.zeros_like(cacc)
    hacc[...] = jnp.zeros_like(hacc)
    with scope("dyA"):
        dy_cp[0].wait_recv()
        for d in (1, 2, 3):
            z_dy(0, d, z).start()

    def step(i, carry):
        @pl.when(i < NC)
        def _():
            with scope("wfwd"):
                wring(i).forward()

        @pl.when(i < NC - LEAD)
        def _():
            wown(i + LEAD)

        @pl.when(i == 0)
        def _():
            with scope("dyB"):
                take(lhs.at[pl.ds(0, 160), pl.ds(0, 512)], y_r.at[1])
                for d in (1, 2, 3):
                    z_dy(1, d, z).start()
            with scope("e1x"):
                local_wait(1)
                take(e1.at[pl.ds(0, 3 * VAL), :], e_r.at[0])
                for n in range(4):
                    e1_y(n, yh).start()
                local_wait(5)
                for cp in v_cp:
                    cp.start()

        @pl.when(i == 2)
        def _():
            with scope("e1y"):
                take(e1.at[pl.ds(0, 4 * VAL), :], e_r.at[1])
                for n in range(4):
                    e1_sib(n, k).start()

        @pl.when((i >= 3) & (i < NC + 3))
        def _():
            with scope("wlast"):
                wring(i - 3).last()

        @pl.when(i == 3)
        def _():
            with scope("e1full"):
                take(e1.at[pl.ds(0, 4 * BW), :], e_r.at[2])
                local_wait(3)
            with scope("iogram"):
                gi = dot_t(e1[:, 0:512], tx[...])
                go = dot_t(e1[:, 512:1024], tdy[...])
                for p in range(8):
                    iop[p, 0] = gi[p * 64 : p * 64 + 64]
                    iop[p, 1] = go[p * 64 : p * 64 + 64]
                for d in (1, 2, 3):
                    z_rs(d).start()

        @pl.when(i == NC - 1)
        def _():
            with scope("vown"):
                take(vv.at[pl.ds(0, VAL), :], y_r.at[2])
                varing.own()
                vbring.own()

        @pl.when(i == 3)
        def _():
            with scope("zdy"):
                local_wait(0)
                local_wait(2)
                take(lhs.at[pl.ds(0, 288), pl.ds(0, 1536)], z_r.at[0])

        with scope("part"):
            @pl.when((i >= 3) & (i < NC + 3))
            def _():
                partial_stage(i - 3)

        @pl.when(i == 10)
        def _():
            with scope("vgfwd"):
                varing.forward()

        @pl.when(i == 7)
        def _():
            with scope("iors"):
                take(ior, z_r.at[1])
                ios[...] = iop[pl.ds(z * 2, 2)] + ior[0] + ior[1] + ior[2]
                iosb[...] = ios[1 - yl].astype(BF)
                yl_rs().start()

        @pl.when(i == 5)
        def _():
            local_wait(4)

        @pl.when((i >= 7) & (i < NC + 7))
        def _():
            with scope("grad"):
                grad_stage(i - 7)

        @pl.when(i == 10)
        def _():
            with scope("vbfwd"):
                vbring.forward()

        @pl.when(i >= 10)
        def _():
            with scope("vcfwd"):
                vcring(i - 10).forward()

        @pl.when(i == 11)
        def _():
            with scope("ylrs"):
                yl_rs().wait_recv()
                iof[z * 2 + yl] = (ios[yl] + ioy[...].astype(F32)).astype(BF)
                yl_ag(yl).start()

        @pl.when(i == NC + 6)
        def _():
            with scope("ylag"):
                yl_ag(1 - yl).wait_recv()
                for d in (1, 2, 3):
                    z_ag(d, z).start()

        return carry

    lax.fori_loop(0, NC + 7, step, 0)
    with scope("tailA"):
        vcring(4).forward()
        varing.last()
        for m in range(4):
            vcring(m).last()
        varing.full()
    for m in range(NC):
        with scope("tail"):
            if m == 1:
                vcring(5).forward()
            if m == 2:
                vbring.last()
                vcring(6).forward()
            if m == 3:
                vcring(4).last()
            if m == 4:
                vbring.full()
                vcring(5).last()
            if m == 5:
                vcring(6).last()
        with scope("gram"):
            gram_stage(m)

    with scope("zag"):
        take(iof.at[pl.ds(0, 6)], z_r.at[2])
    for v in (0, 1):
        acc = jnp.zeros((VAL, TOK), F32)
        for p in range(8):
            r = slice(p * 64 + v * VAL, p * 64 + v * VAL + VAL)
            q = slice(v * VAL, v * VAL + VAL)
            acc += iof[p, 0, q, :].astype(F32) * cacc[r, :] + iof[p, 1, q, :].astype(F32) * hacc[r, :]
        acc = acc[:, 0:128] + acc[:, 128:256]
        acc = acc[0:8] + acc[8:16] + acc[16:24] + acc[24:32]
        fin_s[v * 4 : v * 4 + 4, :] = acc[0:4] + acc[4:8]
    for n, to in enumerate(hids):
        remote(fin_s, fin_r.at[n], f_s, f_r, to).start()
    take(wbuf.at[pl.ds(0, 49 * 32), :], ring_s.at[0])
    take(vc.at[pl.ds(0, 7 * BW), :], ring_s.at[1])
    take(vv.at[pl.ds(0, 7 * BW), :], ring_s.at[2])
    take(e1.at[pl.ds(0, 480), :], e_s)
    take(lhs.at[pl.ds(0, 288), pl.ds(0, 512)], y_s.at[0])
    take(vv.at[pl.ds(0, VAL), :], y_s.at[1])
    take(psend, p_s)
    take(lhs.at[pl.ds(0, 288), pl.ds(0, 1536)], z_s.at[0])
    take(ior, z_s.at[1])
    take(iof.at[pl.ds(0, 6)], z_s.at[2])
    take(iosb, z_s.at[3])
    take(ioy, z_s.at[4])
    with scope("finwait"):
        take(fin_r, f_r)
        take(fin_r, f_s)
    total = fin_s[...]
    for n in range(7):
        total = total + fin_r[n]
    total_o[...] = total


def publish(gg, ug, total, gg_o, ug_o, sc_o, sem):
    rows = TOK // PIECES
    cps = []
    for q in range(PIECES):
        at = pl.ds(q * rows, rows)
        for n, (src, dst) in enumerate(((gg, gg_o), (ug, ug_o))):
            cps.append(pltpu.make_async_copy(src.at[at, :], dst.at[at, :], sem.at[n, q]))
    for cp in cps:
        cp.start()
    scale = -step_rate / (LEN * LEN)
    s0 = jnp.sum(total[0:4, :]) * scale
    s1 = jnp.sum(total[4:8, :]) * scale
    lane = lax.broadcasted_iota(jnp.int32, (1, 2), 1)
    sc_o[...] = jnp.where(lane == 0, s0, s1)
    for cp in cps:
        cp.wait()


def per_device(*args):
    vm = pltpu.VMEM
    dma = pltpu.SemaphoreType.DMA
    hbm = pl.BlockSpec(memory_space=pl.ANY)
    vmem = pl.BlockSpec(memory_space=pltpu.VMEM)
    outs = pl.pallas_call(
        kernel,
        out_shape=(vm((TOK, FFL), BF), vm((TOK, FFL), BF), vm((8, 128), F32)),
        in_specs=[hbm] * 9,
        out_specs=(vmem, vmem, vmem),
        scratch_shapes=[
            vm((FFL, KH), BF),
            vm((576, KH), BF),
            vm((TOK, 512), BF),
            vm((TOK, 512), BF),
            vm((TOK, FFL), BF),
            vm((TOK, FFL), BF),
            vm((512, 1024), BF),
            vm((512, VA + VB), BF),
            vm((512, FFL), BF),
            vm((NC, 320, FC), F32),
            vm((NC, 320, FC), BF),
            vm((NC, 320, FC), BF),
            vm((TOK, FFL), BF),
            vm((8, 2, 64, TOK), F32),
            vm((3, 2, 2, 64, TOK), F32),
            vm((2, 2, 64, TOK), F32),
            vm((2, 64, TOK), BF),
            vm((2, 64, TOK), BF),
            vm((8, 2, 64, TOK), BF),
            vm((512, TOK), F32),
            vm((512, TOK), F32),
            vm((8, 128), F32),
            vm((7, 8, 128), F32),
            dma((6,)),
            dma((3,)),
            dma((2 * NC + 2, 3)),
            dma,
            dma((3,)),
            dma((2,)),
            dma((3,)),
            dma,
            dma((NC,)),
            dma((5,)),
            dma((5,)),
            dma,
            dma,
        ],
        compiler_params=pltpu.CompilerParams(
            collective_id=0, has_side_effects=True, vmem_limit_bytes=56 * 1024 * 1024
        ),
    )(*args)
    outs = [pltpu.with_memory_space_constraint(o, pltpu.VMEM) for o in outs]
    return pl.pallas_call(
        publish,
        out_shape=(
            jax.ShapeDtypeStruct((TOK, FFL), BF),
            jax.ShapeDtypeStruct((TOK, FFL), BF),
            jax.ShapeDtypeStruct((1, 2), F32),
        ),
        in_specs=[vmem, vmem, vmem],
        out_specs=(hbm, hbm, vmem),
        scratch_shapes=[dma((2, PIECES))],
    )(*outs)


def solution(mesh):
    return jax.shard_map(
        per_device,
        mesh=mesh,
        in_specs=(
            P("dp", "hid"),
            P("dp", "hid"),
            P("dp", "hid"),
            P("dp", None),
            P("dp", "hid"),
            P("dp", "hid"),
            P("dp", "hid"),
            P("dp", None),
            P("hid", "dp"),
        ),
        out_specs=(P("dp", "hid"), P("dp", "hid"), P("dp", None)),
        check_vma=False,
    )
```

```python
import functools

import jax
import jax.numpy as jnp
from jax import lax
from jax.experimental import pallas as pl
from jax.experimental.pallas import tpu as pltpu
from jax.sharding import PartitionSpec as P

LEN = 256
step_rate = 0.1
MESH = pl.DeviceIdType.MESH
scope = jax.named_scope
BF = jnp.bfloat16
F32 = jnp.float32

TOK = 256
VAL = 32
FFL = 1792
FC = 256
NC = FFL // FC
KH = 2048
PIECES = 4
LEAD = 3
VA, VB = 8 * FC, 6 * FC
BW = 64


def dot_t(a, b):
    return lax.dot_general(a, b, (((1,), (1,)), ((), ())), preferred_element_type=F32)


def parts(cot, gate, up):
    a = gate.astype(F32)
    b = up.astype(F32)
    s = jax.nn.sigmoid(a)
    silu = a * s
    hidden = (silu * b).astype(BF)
    gate_grad = (cot * b * s * (1.0 + a * (1.0 - s))).astype(BF)
    up_grad = (cot * silu).astype(BF)
    return hidden, gate_grad, up_grad


def kernel(
    tx_h, gate_h, up_h, dy_h, vx_h, vg_h, vu_h, vdy_h, w_h,
    gg, ug, total_o,
    wbuf, lhs, tx, tdy, gate, up, e1, vv, vc, ownp, psend, precv, hd,
    iop, ior, ios, iosb, ioy, iof, iofb, iofo, cacc, hacc, fin_s, fin_r,
    lsem, ring_s, ring_r, e_s, e_r, y_s, y_r, p_s, p_r, z_s, z_r, f_s, f_r,
):
    i_dp = lax.axis_index("dp")
    i_hid = lax.axis_index("hid")
    yh, x, k = i_dp // 8, (i_dp // 2) % 4, i_dp % 2
    yl, z = i_hid // 4, i_hid % 4
    xm, xp, x2 = (x + 3) % 4, (x + 1) % 4, (x + 2) % 4

    def dev(yh_=yh, x_=x, k_=k, yl_=yl, z_=z):
        return ((yh_ * 4 + x_) * 2 + k_, yl_ * 4 + z_)

    right, left, sib = dev(x_=xp), dev(x_=xm), dev(k_=1 - k)
    ypart, cross, ylp = dev(yh_=1 - yh), dev(yh_=1 - yh, yl_=1 - yl), dev(yl_=1 - yl)
    zdev = [dev(z_=(z + d) % 4) for d in (1, 2, 3)]
    hids = zdev + [dev(yl_=1 - yl, z_=(z + d) % 4) for d in range(4)]

    def remote(src, dst, ss, rs, to):
        return pltpu.make_async_remote_copy(
            src_ref=src, dst_ref=dst, send_sem=ss, recv_sem=rs, device_id=to, device_id_type=MESH
        )

    me_blk = x * 2 + k
    own_rows = pl.ds(pl.multiple_of(me_blk * BW + yh * VAL, VAL), VAL)
    half_cols = pl.ds(pl.multiple_of(yh * KH, KH), KH)
    hid_cols = pl.ds(pl.multiple_of(i_hid * 512, 512), 512)
    wcol = pl.ds(pl.multiple_of(me_blk * 256, 256), 256)
    local = [
        (0, w_h, wbuf.at[:, wcol]),
        (1, vx_h, e1.at[own_rows, pl.ds(0, 512)]),
        (1, vdy_h.at[:, hid_cols], e1.at[own_rows, pl.ds(512, 512)]),
        (2, dy_h.at[:, half_cols], lhs.at[pl.ds(0, TOK), :]),
        (2, vdy_h.at[:, half_cols], lhs.at[pl.ds(TOK, VAL), :]),
        (3, tx_h, tx),
        (3, dy_h.at[:, hid_cols], tdy),
        (4, gate_h, gate),
        (4, up_h, up),
    ]
    for c in range(NC):
        for n, src in enumerate((vg_h, vu_h)):
            at = pl.ds((2 * c + n) * FC, FC)
            local.append((5, src.at[:, pl.ds(c * FC, FC)], vv.at[own_rows, at]))
    for n, src, dst in local:
        pltpu.make_async_copy(src, dst, lsem.at[n]).start()

    def take(ref, sem):
        pltpu.make_async_copy(ref, ref, sem).wait()

    local_bytes = (
        wbuf.at[:, pl.ds(0, 256)],
        e1.at[pl.ds(0, VAL), :],
        lhs.at[pl.ds(0, TOK + VAL), :],
        lhs.at[pl.ds(0, 128), :],
        vc,
        vv.at[pl.ds(0, VAL), :],
    )

    def local_wait(n):
        take(local_bytes[n], lsem.at[n])

    barrier = pltpu.get_barrier_semaphore()
    greet = [right, left, dev(x_=x2), sib, ypart, cross] + hids
    for to in greet:
        pl.semaphore_signal(barrier, inc=1, device_id=to, device_id_type=MESH)
    with scope("barrier"):
        pl.semaphore_wait(barrier, len(greet))

    class Ring:
        def __init__(self, kind, slot, view, half, size):
            self.kind, self.slot, self.view, self.half, self.size = kind, slot, view, half, size

        def send(self, n, ref, to, src=None):
            remote(
                ref if src is None else src, ref, ring_s.at[self.kind], ring_r.at[self.slot, n], to
            ).start()

        def own(self, src=None):
            for n, to in ((0, right), (0, left), (2, sib)):
                self.send(n, self.view(x, k), to, src)

        def forward(self):
            take(self.size(2), ring_r.at[self.slot, 0])
            self.send(1, self.half(xm, k, 0), right)
            self.send(1, self.half(xp, k, 1), left)
            self.send(2, self.view(xm, k), sib)
            self.send(2, self.view(xp, k), sib)

        def last(self):
            take(self.size(1), ring_r.at[self.slot, 1])
            self.send(2, self.view(x2, k), sib)

        def full(self):
            take(self.size(4), ring_r.at[self.slot, 2])

    def wring(s):
        def view(xx, kk):
            return wbuf.at[
                pl.ds(pl.multiple_of(s * FC, FC), FC),
                pl.ds(pl.multiple_of((xx * 2 + kk) * 256, 256), 256),
            ]

        def half(xx, kk, n):
            return wbuf.at[
                pl.ds(pl.multiple_of(s * FC + n * (FC // 2), FC // 2), FC // 2),
                pl.ds(pl.multiple_of((xx * 2 + kk) * 256, 256), 256),
            ]

        def size(n):
            return wbuf.at[pl.ds(0, n * FC), pl.ds(0, 256)]

        return Ring(0, s, view, half, size)

    def vring(kind, slot, buf, first, width):
        def rows(xx, kk):
            return pl.ds(pl.multiple_of((xx * 2 + kk) * BW, BW), BW)

        def view(xx, kk):
            return buf.at[rows(xx, kk), pl.ds(first, width)]

        def half(xx, kk, n):
            return buf.at[rows(xx, kk), pl.ds(first + n * (width // 2), width // 2)]

        def size(n):
            return buf.at[pl.ds(0, n * BW), pl.ds(0, width)]

        return Ring(kind, slot, view, half, size)

    def vcring(s):
        return vring(1, NC + s, vc, pl.multiple_of(s * FC, FC // 2), FC)

    varing = vring(2, 2 * NC, vv, 0, VA)
    vbring = vring(2, 2 * NC + 1, vv, VA, VB)

    def wown(s):
        wring(s).own(w_h.at[pl.ds(pl.multiple_of(s * FC, FC), FC), :])

    other_cols = pl.ds(pl.multiple_of((1 - yh) * KH + z * 512, 512), 512)
    zcol = pl.ds(pl.multiple_of(z * 512, 512), 512)

    def yh_cp(n, src, dst, to):
        return remote(src, dst, y_s.at[n // 3], y_r.at[n], to)

    def e1_blk(xx, kk, half_, n):
        rows = pl.multiple_of((xx * 2 + kk) * BW + half_ * VAL, VAL)
        return e1.at[pl.ds(rows, n), :]

    xdev = (right, left, dev(x_=x2))
    xsrc = (xm, xp, x2)

    def e1_x(d, n):
        src = vx_h if n == 0 else vdy_h.at[:, hid_cols]
        return remote(
            src, e1.at[own_rows, pl.ds(n * 512, 512)], e_s, e_r.at[0], xdev[d]
        )

    e1_cp = [e1_x(d, n) for d in range(3) for n in range(2)]

    def e1_y(n, who):
        xx = (x, xm, xp, x2)[n]
        ref = e1_blk(xx, k, who, VAL)
        return remote(ref, ref, e_s, e_r.at[1], ypart)

    def e1_sib(n, kk):
        xx = (x, xm, xp, x2)[n]
        ref = e1_blk(xx, kk, 0, BW)
        return remote(ref, ref, e_s, e_r.at[2], sib)

    pieces = ((0, 64), (64, 96), (160, 96))
    dy_cp = [
        yh_cp(n, dy_h.at[pl.ds(a, r), other_cols], lhs.at[pl.ds(288 + a, r), zcol], cross)
        for n, (a, r) in enumerate(pieces)
    ]
    dy_cp.append(yh_cp(2, vdy_h.at[:, other_cols], lhs.at[pl.ds(544, VAL), zcol], cross))
    v_cp = [
        yh_cp(3, vv.at[own_rows, pl.ds(0, VA)], vv.at[own_rows, pl.ds(0, VA)], ypart),
        yh_cp(3, vv.at[own_rows, pl.ds(VA, VB)], vv.at[own_rows, pl.ds(VA, VB)], ypart),
    ]
    for cp in dy_cp + e1_cp:
        cp.start()
    for c in range(LEAD):
        wown(c)

    def z_dy(n, d, zz):
        ref = lhs.at[
            pl.ds(288 + (0, 64, 160)[n], (64, 96, 128)[n]),
            pl.ds(pl.multiple_of(zz * 512, 512), 512),
        ]
        return remote(ref, ref, z_s.at[0], z_r.at[0], zdev[d - 1])

    def z_rs(d):
        to = (z + d) % 4
        return remote(
            iop.at[pl.ds(to * 2, 2)], ior.at[d - 1], z_s.at[1], z_r.at[1], zdev[d - 1]
        )

    def z_ag(d):
        ref = iof.at[z * 2 + yl]
        return remote(ref, ref, z_s.at[2], z_r.at[2], zdev[d - 1])

    def yl_half():
        return remote(iosb, ioy, z_s.at[3], z_r.at[3], ylp)

    def yl_all():
        return remote(iofb, iofo, z_s.at[4], z_r.at[4], ylp)

    def part_cp(s):
        return remote(psend.at[s], precv.at[s], p_s, p_r.at[s], ypart)

    def cols(s):
        return pl.ds(pl.multiple_of(s * FC, FC), FC)

    def partial_stage(s):
        with scope("wfull"):
            wring(s).full()
        res = dot_t(lhs[...], wbuf[cols(s), :])
        psend[s, 0:288, :] = res[288:576].astype(BF)
        psend[s, 288:320, :] = res[256:288].astype(BF)
        ownp[s, 0:288, :] = res[0:288]
        ownp[s, 288:320, :] = res[544:576]
        part_cp(s).start()

    def grad_stage(s):
        with scope("gradwait"):
            part_cp(s).wait_recv()
        vcot = ownp[s, 256:320, :] + precv[s, 256:320, :].astype(F32)
        base = me_blk * BW
        vc[pl.ds(pl.multiple_of(base + yh * VAL, VAL), VAL), cols(s)] = vcot[0:32].astype(BF)
        vc[pl.ds(pl.multiple_of(base + (1 - yh) * VAL, VAL), VAL), cols(s)] = vcot[32:64].astype(BF)
        cot = ownp[s, 0:256, :] + precv[s, 0:256, :].astype(F32)
        h, g, u = parts(cot, gate[:, cols(s)], up[:, cols(s)])
        hd[:, cols(s)] = h
        gg[:, cols(s)] = g
        ug[:, cols(s)] = u
        vcring(s).own()

    def gram_stage(s):
        vcring(s).full()
        g_at, u_at = pl.multiple_of(s * 2 * FC, FC), pl.multiple_of(s * 2 * FC + FC, FC)
        h, g, u = parts(
            vc[:, cols(s)].astype(F32), vv[:, pl.ds(g_at, FC)], vv[:, pl.ds(u_at, FC)]
        )
        cacc[...] += dot_t(g, gg[:, cols(s)]) + dot_t(u, ug[:, cols(s)])
        hacc[...] += dot_t(h, hd[:, cols(s)])

    cacc[...] = jnp.zeros_like(cacc)
    hacc[...] = jnp.zeros_like(hacc)
    for n in (0, 1):
        with scope("dyA"):
            dy_cp[n].wait_recv()
            for d in (1, 2, 3):
                z_dy(n, d, z).start()

    def step(i, carry):
        @pl.when(i < NC)
        def _():
            with scope("wfwd"):
                wring(i).forward()

        @pl.when(i < NC - LEAD)
        def _():
            wown(i + LEAD)

        @pl.when(i == 0)
        def _():
            with scope("dyB"):
                take(lhs.at[pl.ds(0, 128), pl.ds(0, 512)], y_r.at[2])
                for d in (1, 2, 3):
                    z_dy(2, d, z).start()
            with scope("e1x"):
                local_wait(1)
                take(e1.at[pl.ds(0, 3 * VAL), :], e_r.at[0])
                for n in range(4):
                    e1_y(n, yh).start()
                local_wait(5)
                for cp in v_cp:
                    cp.start()

        @pl.when(i == 2)
        def _():
            with scope("e1y"):
                take(e1.at[pl.ds(0, 4 * VAL), :], e_r.at[1])
                for n in range(4):
                    e1_sib(n, k).start()

        @pl.when((i >= 3) & (i < NC + 3))
        def _():
            with scope("wlast"):
                wring(i - 3).last()

        @pl.when(i == 3)
        def _():
            with scope("e1full"):
                take(e1.at[pl.ds(0, 4 * BW), :], e_r.at[2])
                local_wait(3)
            with scope("iogram"):
                gi = dot_t(e1[:, 0:512], tx[...])
                go = dot_t(e1[:, 512:1024], tdy[...])
                for p in range(8):
                    iop[p, 0] = gi[p * 64 : p * 64 + 64]
                    iop[p, 1] = go[p * 64 : p * 64 + 64]
                for d in (1, 2, 3):
                    z_rs(d).start()

        @pl.when(i == NC - 1)
        def _():
            with scope("vown"):
                take(vv.at[pl.ds(0, VAL), :], y_r.at[3])
                varing.own()
                vbring.own()

        @pl.when(i == 3)
        def _():
            with scope("zdy"):
                local_wait(0)
                local_wait(2)
                take(lhs.at[pl.ds(0, 288), pl.ds(0, 1536)], z_r.at[0])

        with scope("part"):
            @pl.when((i >= 3) & (i < NC + 3))
            def _():
                partial_stage(i - 3)

        @pl.when(i == 10)
        def _():
            with scope("ylhalf"):
                yl_half().wait_recv()
                iof[z * 2 + yl] = ios[yl] + ioy[...].astype(F32)
                for d in (1, 2, 3):
                    z_ag(d).start()
            with scope("vgfwd"):
                varing.forward()

        @pl.when(i == 7)
        def _():
            with scope("iors"):
                take(ior, z_r.at[1])
                ios[...] = iop[pl.ds(z * 2, 2)] + ior[0] + ior[1] + ior[2]
                iosb[...] = ios[1 - yl].astype(BF)
                yl_half().start()

        @pl.when(i == 5)
        def _():
            local_wait(4)

        @pl.when((i >= 7) & (i < NC + 7))
        def _():
            with scope("grad"):
                grad_stage(i - 7)

        @pl.when(i == 10)
        def _():
            with scope("vbfwd"):
                vbring.forward()

        @pl.when(i >= 10)
        def _():
            with scope("vcfwd"):
                vcring(i - 10).forward()

        @pl.when(i == NC + 6)
        def _():
            with scope("zag"):
                take(iof.at[pl.ds(0, 3)], z_r.at[2])
                for q in range(4):
                    iofb[q] = iof[q * 2 + yl].astype(BF)
                yl_all().start()

        return carry

    lax.fori_loop(0, NC + 7, step, 0)
    with scope("tailA"):
        vcring(4).forward()
        vcring(5).forward()
        varing.last()
        for m in range(4):
            vcring(m).last()
        varing.full()
    for m in range(NC):
        with scope("tail%d" % m):
            if m == 1:
                vcring(6).forward()
                vbring.last()
            if m == 3:
                vcring(4).last()
                vcring(5).last()
            if m == 4:
                vbring.full()
            if m == 5:
                vcring(6).last()
        with scope("gram"):
            gram_stage(m)

    with scope("ylall"):
        yl_all().wait_recv()
    for v in (0, 1):
        acc = jnp.zeros((VAL, TOK), F32)
        at = slice(v * VAL, v * VAL + VAL)
        for q in range(4):
            for who in (0, 1):
                side = yl if who == 0 else 1 - yl
                r = pl.ds(pl.multiple_of((q * 2 + side) * BW + v * VAL, VAL), VAL)
                if who == 0:
                    gi, go = iof[q * 2 + yl, 0, at, :], iof[q * 2 + yl, 1, at, :]
                else:
                    gi, go = iofo[q, 0, at, :].astype(F32), iofo[q, 1, at, :].astype(F32)
                acc += gi * cacc[r, :] + go * hacc[r, :]
        acc = acc[:, 0:128] + acc[:, 128:256]
        acc = acc[0:8] + acc[8:16] + acc[16:24] + acc[24:32]
        fin_s[v * 4 : v * 4 + 4, :] = acc[0:4] + acc[4:8]
    for n, to in enumerate(hids):
        remote(fin_s, fin_r.at[n], f_s, f_r, to).start()
    take(wbuf.at[pl.ds(0, 49 * 32), :], ring_s.at[0])
    take(vc.at[pl.ds(0, 7 * BW), :], ring_s.at[1])
    take(vv.at[pl.ds(0, 7 * BW), :], ring_s.at[2])
    take(e1.at[pl.ds(0, 480), :], e_s)
    take(lhs.at[pl.ds(0, 288), pl.ds(0, 512)], y_s.at[0])
    take(vv.at[pl.ds(0, VAL), :], y_s.at[1])
    take(psend, p_s)
    take(lhs.at[pl.ds(0, 288), pl.ds(0, 1536)], z_s.at[0])
    take(ior, z_s.at[1])
    take(iof.at[pl.ds(0, 3)], z_s.at[2])
    take(iosb, z_s.at[3])
    take(iofb, z_s.at[4])
    with scope("finwait"):
        take(fin_r, f_r)
        take(fin_r, f_s)
    total = fin_s[...]
    for n in range(7):
        total = total + fin_r[n]
    total_o[...] = total


def publish(gg, ug, total, gg_o, ug_o, sc_o, sem):
    rows = TOK // PIECES
    cps = []
    for q in range(PIECES):
        at = pl.ds(q * rows, rows)
        for n, (src, dst) in enumerate(((gg, gg_o), (ug, ug_o))):
            cps.append(pltpu.make_async_copy(src.at[at, :], dst.at[at, :], sem.at[n, q]))
    for cp in cps:
        cp.start()
    scale = -step_rate / (LEN * LEN)
    s0 = jnp.sum(total[0:4, :]) * scale
    s1 = jnp.sum(total[4:8, :]) * scale
    lane = lax.broadcasted_iota(jnp.int32, (1, 2), 1)
    sc_o[...] = jnp.where(lane == 0, s0, s1)
    for cp in cps:
        cp.wait()


def per_device(*args):
    vm = pltpu.VMEM
    dma = pltpu.SemaphoreType.DMA
    hbm = pl.BlockSpec(memory_space=pl.ANY)
    vmem = pl.BlockSpec(memory_space=pltpu.VMEM)
    outs = pl.pallas_call(
        kernel,
        out_shape=(vm((TOK, FFL), BF), vm((TOK, FFL), BF), vm((8, 128), F32)),
        in_specs=[hbm] * 9,
        out_specs=(vmem, vmem, vmem),
        scratch_shapes=[
            vm((FFL, KH), BF),
            vm((576, KH), BF),
            vm((TOK, 512), BF),
            vm((TOK, 512), BF),
            vm((TOK, FFL), BF),
            vm((TOK, FFL), BF),
            vm((512, 1024), BF),
            vm((512, VA + VB), BF),
            vm((512, FFL), BF),
            vm((NC, 320, FC), F32),
            vm((NC, 320, FC), BF),
            vm((NC, 320, FC), BF),
            vm((TOK, FFL), BF),
            vm((8, 2, 64, TOK), F32),
            vm((3, 2, 2, 64, TOK), F32),
            vm((2, 2, 64, TOK), F32),
            vm((2, 64, TOK), BF),
            vm((2, 64, TOK), BF),
            vm((8, 2, 64, TOK), F32),
            vm((4, 2, 64, TOK), BF),
            vm((4, 2, 64, TOK), BF),
            vm((512, TOK), F32),
            vm((512, TOK), F32),
            vm((8, 128), F32),
            vm((7, 8, 128), F32),
            dma((6,)),
            dma((3,)),
            dma((2 * NC + 2, 3)),
            dma,
            dma((3,)),
            dma((2,)),
            dma((4,)),
            dma,
            dma((NC,)),
            dma((5,)),
            dma((5,)),
            dma,
            dma,
        ],
        compiler_params=pltpu.CompilerParams(
            collective_id=0, has_side_effects=True, vmem_limit_bytes=56 * 1024 * 1024
        ),
    )(*args)
    outs = [pltpu.with_memory_space_constraint(o, pltpu.VMEM) for o in outs]
    return pl.pallas_call(
        publish,
        out_shape=(
            jax.ShapeDtypeStruct((TOK, FFL), BF),
            jax.ShapeDtypeStruct((TOK, FFL), BF),
            jax.ShapeDtypeStruct((1, 2), F32),
        ),
        in_specs=[vmem, vmem, vmem],
        out_specs=(hbm, hbm, vmem),
        scratch_shapes=[dma((2, PIECES))],
    )(*outs)


def solution(mesh):
    return jax.shard_map(
        per_device,
        mesh=mesh,
        in_specs=(
            P("dp", "hid"),
            P("dp", "hid"),
            P("dp", "hid"),
            P("dp", None),
            P("dp", "hid"),
            P("dp", "hid"),
            P("dp", "hid"),
            P("dp", None),
            P("hid", "dp"),
        ),
        out_specs=(P("dp", "hid"), P("dp", "hid"), P("dp", None)),
        check_vma=False,
    )
```

```python
import functools

import jax
import jax.numpy as jnp
from jax import lax
from jax.experimental import pallas as pl
from jax.experimental.pallas import tpu as pltpu
from jax.sharding import PartitionSpec as P

LEN = 256
step_rate = 0.1
MESH = pl.DeviceIdType.MESH
scope = jax.named_scope
BF = jnp.bfloat16
F32 = jnp.float32

TOK = 256
VAL = 32
FFL = 1792
FC = 256
NC = FFL // FC
KH = 2048
PIECES = 4
LEAD = 3
VA, VB = 8 * FC, 6 * FC
BW = 64


def dot_t(a, b):
    return lax.dot_general(a, b, (((1,), (1,)), ((), ())), preferred_element_type=F32)


def parts(cot, gate, up):
    a = gate.astype(F32)
    b = up.astype(F32)
    s = jax.nn.sigmoid(a)
    silu = a * s
    hidden = (silu * b).astype(BF)
    gate_grad = (cot * b * s * (1.0 + a * (1.0 - s))).astype(BF)
    up_grad = (cot * silu).astype(BF)
    return hidden, gate_grad, up_grad


def kernel(
    tx_h, gate_h, up_h, dy_h, vx_h, vg_h, vu_h, vdy_h, w_h,
    gg, ug, total_o,
    wbuf, lhs, tx, tdy, gate, up, e1, vv, vc, ownp, psend, precv, hd,
    iop, ior, ios, iosb, ioy, iof, iofb, iofo, cacc, hacc, fin_s, fin_r,
    lsem, ring_s, ring_r, e_s, e_r, y_s, y_r, p_s, p_r, z_s, z_r, f_s, f_r,
):
    i_dp = lax.axis_index("dp")
    i_hid = lax.axis_index("hid")
    yh, x, k = i_dp // 8, (i_dp // 2) % 4, i_dp % 2
    yl, z = i_hid // 4, i_hid % 4
    xm, xp, x2 = (x + 3) % 4, (x + 1) % 4, (x + 2) % 4

    def dev(yh_=yh, x_=x, k_=k, yl_=yl, z_=z):
        return ((yh_ * 4 + x_) * 2 + k_, yl_ * 4 + z_)

    right, left, sib = dev(x_=xp), dev(x_=xm), dev(k_=1 - k)
    ypart, cross, ylp = dev(yh_=1 - yh), dev(yh_=1 - yh, yl_=1 - yl), dev(yl_=1 - yl)
    zdev = [dev(z_=(z + d) % 4) for d in (1, 2, 3)]
    hids = zdev + [dev(yl_=1 - yl, z_=(z + d) % 4) for d in range(4)]

    def remote(src, dst, ss, rs, to):
        return pltpu.make_async_remote_copy(
            src_ref=src, dst_ref=dst, send_sem=ss, recv_sem=rs, device_id=to, device_id_type=MESH
        )

    me_blk = x * 2 + k
    own_rows = pl.ds(pl.multiple_of(me_blk * BW + yh * VAL, VAL), VAL)
    half_cols = pl.ds(pl.multiple_of(yh * KH, KH), KH)
    hid_cols = pl.ds(pl.multiple_of(i_hid * 512, 512), 512)
    wcol = pl.ds(pl.multiple_of(me_blk * 256, 256), 256)
    local = [
        (0, w_h, wbuf.at[:, wcol]),
        (1, vx_h, e1.at[own_rows, pl.ds(0, 512)]),
        (1, vdy_h.at[:, hid_cols], e1.at[own_rows, pl.ds(512, 512)]),
        (2, dy_h.at[:, half_cols], lhs.at[pl.ds(0, TOK), :]),
        (2, vdy_h.at[:, half_cols], lhs.at[pl.ds(TOK, VAL), :]),
        (3, tx_h, tx),
        (3, dy_h.at[:, hid_cols], tdy),
        (4, gate_h, gate),
        (4, up_h, up),
    ]
    for c in range(NC):
        for n, src in enumerate((vg_h, vu_h)):
            at = pl.ds((2 * c + n) * FC, FC)
            local.append((5, src.at[:, pl.ds(c * FC, FC)], vv.at[own_rows, at]))
    for n, src, dst in local:
        pltpu.make_async_copy(src, dst, lsem.at[n]).start()

    def take(ref, sem):
        pltpu.make_async_copy(ref, ref, sem).wait()

    local_bytes = (
        wbuf.at[:, pl.ds(0, 256)],
        e1.at[pl.ds(0, VAL), :],
        lhs.at[pl.ds(0, TOK + VAL), :],
        lhs.at[pl.ds(0, 128), :],
        vc,
        vv.at[pl.ds(0, VAL), :],
    )

    def local_wait(n):
        take(local_bytes[n], lsem.at[n])

    barrier = pltpu.get_barrier_semaphore()
    greet = [right, left, dev(x_=x2), sib, ypart, cross] + hids
    for to in greet:
        pl.semaphore_signal(barrier, inc=1, device_id=to, device_id_type=MESH)
    with scope("barrier"):
        pl.semaphore_wait(barrier, len(greet))

    class Ring:
        def __init__(self, kind, slot, view, half, size):
            self.kind, self.slot, self.view, self.half, self.size = kind, slot, view, half, size

        def send(self, n, ref, to, src=None):
            remote(
                ref if src is None else src, ref, ring_s.at[self.kind], ring_r.at[self.slot, n], to
            ).start()

        def own(self, src=None):
            for n, to in ((0, right), (0, left), (2, sib)):
                self.send(n, self.view(x, k), to, src)

        def forward(self):
            take(self.size(2), ring_r.at[self.slot, 0])
            self.send(1, self.half(xm, k, 0), right)
            self.send(1, self.half(xp, k, 1), left)
            self.send(2, self.view(xm, k), sib)
            self.send(2, self.view(xp, k), sib)

        def last(self):
            take(self.size(1), ring_r.at[self.slot, 1])
            self.send(2, self.view(x2, k), sib)

        def full(self):
            take(self.size(4), ring_r.at[self.slot, 2])

    def wring(s):
        def view(xx, kk):
            return wbuf.at[
                pl.ds(pl.multiple_of(s * FC, FC), FC),
                pl.ds(pl.multiple_of((xx * 2 + kk) * 256, 256), 256),
            ]

        def half(xx, kk, n):
            return wbuf.at[
                pl.ds(pl.multiple_of(s * FC + n * (FC // 2), FC // 2), FC // 2),
                pl.ds(pl.multiple_of((xx * 2 + kk) * 256, 256), 256),
            ]

        def size(n):
            return wbuf.at[pl.ds(0, n * FC), pl.ds(0, 256)]

        return Ring(0, s, view, half, size)

    def vring(kind, slot, buf, first, width):
        def rows(xx, kk):
            return pl.ds(pl.multiple_of((xx * 2 + kk) * BW, BW), BW)

        def view(xx, kk):
            return buf.at[rows(xx, kk), pl.ds(first, width)]

        def half(xx, kk, n):
            return buf.at[rows(xx, kk), pl.ds(first + n * (width // 2), width // 2)]

        def size(n):
            return buf.at[pl.ds(0, n * BW), pl.ds(0, width)]

        return Ring(kind, slot, view, half, size)

    def vcring(s):
        return vring(1, NC + s, vc, pl.multiple_of(s * FC, FC // 2), FC)

    varing = vring(2, 2 * NC, vv, 0, VA)
    vbring = vring(2, 2 * NC + 1, vv, VA, VB)

    def wown(s):
        wring(s).own(w_h.at[pl.ds(pl.multiple_of(s * FC, FC), FC), :])

    other_cols = pl.ds(pl.multiple_of((1 - yh) * KH + z * 512, 512), 512)
    zcol = pl.ds(pl.multiple_of(z * 512, 512), 512)

    def yh_cp(n, src, dst, to):
        return remote(src, dst, y_s.at[n // 3], y_r.at[n], to)

    def e1_blk(xx, kk, half_, n):
        rows = pl.multiple_of((xx * 2 + kk) * BW + half_ * VAL, VAL)
        return e1.at[pl.ds(rows, n), :]

    xdev = (right, left, dev(x_=x2))
    xsrc = (xm, xp, x2)

    def e1_x(d, n):
        src = vx_h if n == 0 else vdy_h.at[:, hid_cols]
        return remote(
            src, e1.at[own_rows, pl.ds(n * 512, 512)], e_s, e_r.at[0], xdev[d]
        )

    e1_cp = [e1_x(d, n) for d in range(3) for n in range(2)]

    def e1_y(n, who):
        xx = (x, xm, xp, x2)[n]
        ref = e1_blk(xx, k, who, VAL)
        return remote(ref, ref, e_s, e_r.at[1], ypart)

    def e1_sib(n, kk):
        xx = (x, xm, xp, x2)[n]
        ref = e1_blk(xx, kk, 0, BW)
        return remote(ref, ref, e_s, e_r.at[2], sib)

    pieces = ((0, 64), (64, 96), (160, 96))
    dy_cp = [
        yh_cp(n, dy_h.at[pl.ds(a, r), other_cols], lhs.at[pl.ds(288 + a, r), zcol], cross)
        for n, (a, r) in enumerate(pieces)
    ]
    dy_cp.append(yh_cp(2, vdy_h.at[:, other_cols], lhs.at[pl.ds(544, VAL), zcol], cross))
    v_cp = [
        yh_cp(3, vv.at[own_rows, pl.ds(0, VA)], vv.at[own_rows, pl.ds(0, VA)], ypart),
        yh_cp(3, vv.at[own_rows, pl.ds(VA, VB)], vv.at[own_rows, pl.ds(VA, VB)], ypart),
    ]
    for cp in dy_cp:
        cp.start()
    wown(0)
    for cp in e1_cp:
        cp.start()
    for c in range(1, LEAD):
        wown(c)

    def z_dy(n, d, zz):
        ref = lhs.at[
            pl.ds(288 + (0, 64, 160)[n], (64, 96, 128)[n]),
            pl.ds(pl.multiple_of(zz * 512, 512), 512),
        ]
        return remote(ref, ref, z_s.at[0], z_r.at[0], zdev[d - 1])

    def z_rs(d):
        to = (z + d) % 4
        return remote(
            iop.at[pl.ds(to * 2, 2)], ior.at[d - 1], z_s.at[1], z_r.at[1], zdev[d - 1]
        )

    def z_ag(d):
        ref = iof.at[z * 2 + yl]
        return remote(ref, ref, z_s.at[2], z_r.at[2], zdev[d - 1])

    def yl_half():
        return remote(iosb, ioy, z_s.at[3], z_r.at[3], ylp)

    def yl_all():
        return remote(iofb, iofo, z_s.at[4], z_r.at[4], ylp)

    def part_cp(s):
        return remote(psend.at[s], precv.at[s], p_s, p_r.at[s], ypart)

    def cols(s):
        return pl.ds(pl.multiple_of(s * FC, FC), FC)

    def partial_stage(s):
        with scope("wfull"):
            wring(s).full()
        res = dot_t(lhs[...], wbuf[cols(s), :])
        psend[s, 0:288, :] = res[288:576].astype(BF)
        psend[s, 288:320, :] = res[256:288].astype(BF)
        ownp[s, 0:288, :] = res[0:288]
        ownp[s, 288:320, :] = res[544:576]
        part_cp(s).start()

    def grad_stage(s):
        with scope("gradwait"):
            part_cp(s).wait_recv()
        vcot = ownp[s, 256:320, :] + precv[s, 256:320, :].astype(F32)
        base = me_blk * BW
        vc[pl.ds(pl.multiple_of(base + yh * VAL, VAL), VAL), cols(s)] = vcot[0:32].astype(BF)
        vc[pl.ds(pl.multiple_of(base + (1 - yh) * VAL, VAL), VAL), cols(s)] = vcot[32:64].astype(BF)
        cot = ownp[s, 0:256, :] + precv[s, 0:256, :].astype(F32)
        h, g, u = parts(cot, gate[:, cols(s)], up[:, cols(s)])
        hd[:, cols(s)] = h
        gg[:, cols(s)] = g
        ug[:, cols(s)] = u
        vcring(s).own()

    def gram_stage(s):
        vcring(s).full()
        g_at, u_at = pl.multiple_of(s * 2 * FC, FC), pl.multiple_of(s * 2 * FC + FC, FC)
        h, g, u = parts(
            vc[:, cols(s)].astype(F32), vv[:, pl.ds(g_at, FC)], vv[:, pl.ds(u_at, FC)]
        )
        cacc[...] += dot_t(g, gg[:, cols(s)]) + dot_t(u, ug[:, cols(s)])
        hacc[...] += dot_t(h, hd[:, cols(s)])

    cacc[...] = jnp.zeros_like(cacc)
    hacc[...] = jnp.zeros_like(hacc)
    for n in (0, 1):
        with scope("dyA"):
            dy_cp[n].wait_recv()
            for d in (1, 2, 3):
                z_dy(n, d, z).start()

    def step(i, carry):
        @pl.when(i < NC)
        def _():
            with scope("wfwd"):
                wring(i).forward()

        @pl.when(i < NC - LEAD)
        def _():
            wown(i + LEAD)

        @pl.when(i == 0)
        def _():
            with scope("dyB"):
                take(lhs.at[pl.ds(0, 128), pl.ds(0, 512)], y_r.at[2])
                for d in (1, 2, 3):
                    z_dy(2, d, z).start()
            with scope("e1x"):
                local_wait(1)
                take(e1.at[pl.ds(0, 3 * VAL), :], e_r.at[0])
                for n in range(4):
                    e1_y(n, yh).start()
                local_wait(5)
                for cp in v_cp:
                    cp.start()

        @pl.when(i == 2)
        def _():
            with scope("e1y"):
                take(e1.at[pl.ds(0, 4 * VAL), :], e_r.at[1])
                for n in range(4):
                    e1_sib(n, k).start()

        @pl.when((i >= 3) & (i < NC + 3))
        def _():
            with scope("wlast"):
                wring(i - 3).last()

        @pl.when(i == 3)
        def _():
            with scope("e1full"):
                take(e1.at[pl.ds(0, 4 * BW), :], e_r.at[2])
                local_wait(3)
            with scope("iogram"):
                gi = dot_t(e1[:, 0:512], tx[...])
                go = dot_t(e1[:, 512:1024], tdy[...])
                for p in range(8):
                    iop[p, 0] = gi[p * 64 : p * 64 + 64]
                    iop[p, 1] = go[p * 64 : p * 64 + 64]
                for d in (1, 2, 3):
                    z_rs(d).start()

        @pl.when(i == NC - 1)
        def _():
            with scope("vown"):
                take(vv.at[pl.ds(0, VAL), :], y_r.at[3])
                varing.own()
                vbring.own()

        @pl.when(i == 3)
        def _():
            with scope("zdy"):
                local_wait(0)
                local_wait(2)
                take(lhs.at[pl.ds(0, 288), pl.ds(0, 1536)], z_r.at[0])

        with scope("part"):
            @pl.when((i >= 3) & (i < NC + 3))
            def _():
                partial_stage(i - 3)

        @pl.when(i == 10)
        def _():
            with scope("ylhalf"):
                yl_half().wait_recv()
                iof[z * 2 + yl] = ios[yl] + ioy[...].astype(F32)
                for d in (1, 2, 3):
                    z_ag(d).start()
            with scope("vgfwd"):
                varing.forward()

        @pl.when(i == 7)
        def _():
            with scope("iors"):
                take(ior, z_r.at[1])
                ios[...] = iop[pl.ds(z * 2, 2)] + ior[0] + ior[1] + ior[2]
                iosb[...] = ios[1 - yl].astype(BF)
                yl_half().start()

        @pl.when(i == 5)
        def _():
            local_wait(4)

        @pl.when((i >= 7) & (i < NC + 7))
        def _():
            with scope("grad"):
                grad_stage(i - 7)

        @pl.when(i == 10)
        def _():
            with scope("vbfwd"):
                vbring.forward()

        @pl.when(i >= 10)
        def _():
            with scope("vcfwd"):
                vcring(i - 10).forward()

        @pl.when(i == NC + 6)
        def _():
            with scope("zag"):
                take(iof.at[pl.ds(0, 3)], z_r.at[2])
                for q in range(4):
                    iofb[q] = iof[q * 2 + yl].astype(BF)
                yl_all().start()

        return carry

    lax.fori_loop(0, NC + 7, step, 0)
    with scope("tailA"):
        vcring(4).forward()
        vcring(5).forward()
        varing.last()
        for m in range(4):
            vcring(m).last()
        varing.full()
    for m in range(NC):
        with scope("tail%d" % m):
            if m == 1:
                vcring(6).forward()
                vbring.last()
            if m == 3:
                vcring(4).last()
                vcring(5).last()
            if m == 4:
                vbring.full()
            if m == 5:
                vcring(6).last()
        with scope("gram"):
            gram_stage(m)

    with scope("ylall"):
        yl_all().wait_recv()
    for v in (0, 1):
        acc = jnp.zeros((VAL, TOK), F32)
        at = slice(v * VAL, v * VAL + VAL)
        for q in range(4):
            for who in (0, 1):
                side = yl if who == 0 else 1 - yl
                r = pl.ds(pl.multiple_of((q * 2 + side) * BW + v * VAL, VAL), VAL)
                if who == 0:
                    gi, go = iof[q * 2 + yl, 0, at, :], iof[q * 2 + yl, 1, at, :]
                else:
                    gi, go = iofo[q, 0, at, :].astype(F32), iofo[q, 1, at, :].astype(F32)
                acc += gi * cacc[r, :] + go * hacc[r, :]
        acc = acc[:, 0:128] + acc[:, 128:256]
        acc = acc[0:8] + acc[8:16] + acc[16:24] + acc[24:32]
        fin_s[v * 4 : v * 4 + 4, :] = acc[0:4] + acc[4:8]
    for n, to in enumerate(hids):
        remote(fin_s, fin_r.at[n], f_s, f_r, to).start()
    take(wbuf.at[pl.ds(0, 49 * 32), :], ring_s.at[0])
    take(vc.at[pl.ds(0, 7 * BW), :], ring_s.at[1])
    take(vv.at[pl.ds(0, 7 * BW), :], ring_s.at[2])
    take(e1.at[pl.ds(0, 480), :], e_s)
    take(lhs.at[pl.ds(0, 288), pl.ds(0, 512)], y_s.at[0])
    take(vv.at[pl.ds(0, VAL), :], y_s.at[1])
    take(psend, p_s)
    take(lhs.at[pl.ds(0, 288), pl.ds(0, 1536)], z_s.at[0])
    take(ior, z_s.at[1])
    take(iof.at[pl.ds(0, 3)], z_s.at[2])
    take(iosb, z_s.at[3])
    take(iofb, z_s.at[4])
    with scope("finwait"):
        take(fin_r, f_r)
        take(fin_r, f_s)
    total = fin_s[...]
    for n in range(7):
        total = total + fin_r[n]
    total_o[...] = total


def publish(gg, ug, total, gg_o, ug_o, sc_o, sem):
    rows = TOK // PIECES
    cps = []
    for q in range(PIECES):
        at = pl.ds(q * rows, rows)
        for n, (src, dst) in enumerate(((gg, gg_o), (ug, ug_o))):
            cps.append(pltpu.make_async_copy(src.at[at, :], dst.at[at, :], sem.at[n, q]))
    for cp in cps:
        cp.start()
    scale = -step_rate / (LEN * LEN)
    s0 = jnp.sum(total[0:4, :]) * scale
    s1 = jnp.sum(total[4:8, :]) * scale
    lane = lax.broadcasted_iota(jnp.int32, (1, 2), 1)
    sc_o[...] = jnp.where(lane == 0, s0, s1)
    for cp in cps:
        cp.wait()


def per_device(*args):
    vm = pltpu.VMEM
    dma = pltpu.SemaphoreType.DMA
    hbm = pl.BlockSpec(memory_space=pl.ANY)
    vmem = pl.BlockSpec(memory_space=pltpu.VMEM)
    outs = pl.pallas_call(
        kernel,
        out_shape=(vm((TOK, FFL), BF), vm((TOK, FFL), BF), vm((8, 128), F32)),
        in_specs=[hbm] * 9,
        out_specs=(vmem, vmem, vmem),
        scratch_shapes=[
            vm((FFL, KH), BF),
            vm((576, KH), BF),
            vm((TOK, 512), BF),
            vm((TOK, 512), BF),
            vm((TOK, FFL), BF),
            vm((TOK, FFL), BF),
            vm((512, 1024), BF),
            vm((512, VA + VB), BF),
            vm((512, FFL), BF),
            vm((NC, 320, FC), F32),
            vm((NC, 320, FC), BF),
            vm((NC, 320, FC), BF),
            vm((TOK, FFL), BF),
            vm((8, 2, 64, TOK), F32),
            vm((3, 2, 2, 64, TOK), F32),
            vm((2, 2, 64, TOK), F32),
            vm((2, 64, TOK), BF),
            vm((2, 64, TOK), BF),
            vm((8, 2, 64, TOK), F32),
            vm((4, 2, 64, TOK), BF),
            vm((4, 2, 64, TOK), BF),
            vm((512, TOK), F32),
            vm((512, TOK), F32),
            vm((8, 128), F32),
            vm((7, 8, 128), F32),
            dma((6,)),
            dma((3,)),
            dma((2 * NC + 2, 3)),
            dma,
            dma((3,)),
            dma((2,)),
            dma((4,)),
            dma,
            dma((NC,)),
            dma((5,)),
            dma((5,)),
            dma,
            dma,
        ],
        compiler_params=pltpu.CompilerParams(
            collective_id=0, has_side_effects=True, vmem_limit_bytes=56 * 1024 * 1024
        ),
    )(*args)
    outs = [pltpu.with_memory_space_constraint(o, pltpu.VMEM) for o in outs]
    return pl.pallas_call(
        publish,
        out_shape=(
            jax.ShapeDtypeStruct((TOK, FFL), BF),
            jax.ShapeDtypeStruct((TOK, FFL), BF),
            jax.ShapeDtypeStruct((1, 2), F32),
        ),
        in_specs=[vmem, vmem, vmem],
        out_specs=(hbm, hbm, vmem),
        scratch_shapes=[dma((2, PIECES))],
    )(*outs)


def solution(mesh):
    return jax.shard_map(
        per_device,
        mesh=mesh,
        in_specs=(
            P("dp", "hid"),
            P("dp", "hid"),
            P("dp", "hid"),
            P("dp", None),
            P("dp", "hid"),
            P("dp", "hid"),
            P("dp", "hid"),
            P("dp", None),
            P("hid", "dp"),
        ),
        out_specs=(P("dp", "hid"), P("dp", "hid"), P("dp", None)),
        check_vma=False,
    )
```
